32 devices in a mesh: seq: 16 (over z, y, core), mp: 2 (over x).
Axes of the slice: x: 2, y: 2, z: 4, core: 2. Of those that a mesh axis runs over, the one named last changes fastest.
Arguments:
- hidden: bfloat16 [4096, 2048], P('seq'), may hold values from -6 to 6
- ids: int32 [4096], P('seq'), may hold values from 0 to 4, as said below
- w_value: bfloat16 [2048, 2048], P(None, 'mp'), may hold values from -0.125 to 0.125
- w_bc: bfloat16 [2048, 2, 64], P(None, 'mp'), may hold values from -0.015625 to 0.015625
- w_step: bfloat16 [2048, 16], P(None, 'mp'), may hold values from -0.125 to 0.125
- step_bias: float32 [16], P('mp'), may hold values from -1 to 1
- decay_log: float32 [16], P('mp'), may hold values from -12 to -2
- skip: float32 [16], P('mp'), may hold values from 0.5 to 1.5
- norm_gain: float32 [2048], P('mp'), may hold values from 0.1 to 1.9
- w_out: bfloat16 [2048, 2048], P('mp'), may hold values from -0.125 to 0.125
- cotangent: bfloat16 [4096, 2048], P('seq'), may hold values from -6 to 6
Outputs:
- out: bfloat16 [4096, 2048], P('seq', 'mp')
- d_hidden: bfloat16 [4096, 2048], P('seq', 'mp')
The draws below stay inside these ranges and needn't reach their ends.
Inputs may be any that keep to these rules, and one draw needn't show every extreme that they name: `ids`: 4 marks an unknown base (N); such bases come in runs.
All inputs are finite; a program needn't handle non-finite values.
Results may differ from the reference program's by a relative error of at most 0.014.
Values may be sent and summed in bfloat16 or wider, within the bound.
A program may use at most 320 MiB of HBM per device.

```python
from functools import partial
import jax
import jax.numpy as jnp
from jax import lax

D = 2048
HEADS = 16
HEAD_DIM = 128
STATE = 32
GROUPS = 2
RUNS = 4
L_DEV = 256
INNER = 2048
TOTAL = 4096


def draw_ids(key, part):
    key_bases, key_starts, key_lengths = jax.random.split(key, 3)
    bases = jax.random.randint(key_bases, (TOTAL,), 0, 4)
    starts = jax.random.randint(key_starts, (RUNS,), 0, TOTAL)
    lengths = jax.random.randint(key_lengths, (RUNS,), 1, 2 * L_DEV)
    position = jnp.arange(TOTAL)
    inside = (position[None, :] >= starts[:, None]) & (position[None, :] < starts[:, None] + lengths[:, None])
    return jnp.where(jnp.any(inside, axis=0), 4, bases).astype(jnp.int32)


def draw_decay_log(key, part):
    key_kind, key_slow, key_fast = jax.random.split(key, 3)
    slow_heads = jax.random.uniform(key_kind, (HEADS,)) < 0.5
    slow_rate = jax.random.uniform(key_slow, (HEADS,), minval=0.3, maxval=1.5) / TOTAL
    fast_rate = jax.random.uniform(key_fast, (HEADS,), minval=0.02, maxval=0.05)
    return jnp.log(jnp.where(slow_heads, slow_rate, fast_rate)).astype(jnp.float32)


def levels(key, extent, cuts, low, top_value):
    gain, own = 1.0, jax.random.fold_in(key, 6)
    for axis_at, blocks in cuts:
        draws = jnp.exp(jax.random.uniform(jax.random.fold_in(own, axis_at), (blocks,), jnp.float32, low / len(cuts), top_value / len(cuts)))
        gain = gain * jnp.repeat(draws, extent[axis_at] // blocks).reshape([-1 if axis == axis_at else 1 for axis in range(len(extent))])
    return gain


def bell_draw(own_key, shape, scale, limit, shards=(), held_as=jnp.bfloat16):
    values = scale * jax.random.normal(own_key, shape, jnp.float32)
    if shards:
        values = values * levels(own_key, shape, shards, -0.22, 0.18)
    return jnp.clip(values, -limit, limit).astype(held_as)


def setup_inputs(seed: int = 0) -> dict:
    key_of = jax.random.split(jax.random.key(seed), 12)
    hidden = bell_draw(key_of[0], (TOTAL, D), 1.0, 6.0, ((0, 16),))
    ids = draw_ids(jax.random.fold_in(key_of[11], 71), 0)
    w_value = bell_draw(key_of[2], (D, INNER), D ** -0.5, 0.125, ((1, 2),))
    w_bc = bell_draw(key_of[3], (D, GROUPS, 2 * STATE), (D * 64) ** -0.5, 0.015625, ((1, 2),))
    w_step = bell_draw(key_of[4], (D, HEADS), D ** -0.5, 0.125, ((1, 2),))
    step_bias = jnp.clip(jax.random.uniform(key_of[5], (HEADS,), jnp.float32, -1.0, 1.0) * levels(key_of[5], (HEADS,), ((0, 2),), -0.4, 0.0), -1.0, 1.0)
    decay_log = draw_decay_log(jax.random.fold_in(key_of[11], 71), 0)
    skip = jnp.clip(0.5 + 1.0 * jax.random.uniform(key_of[7], (HEADS,), jnp.float32) ** levels(key_of[7], (HEADS,), ((0, 2),), -0.2, 0.2), 0.5, 1.5)
    norm_gain = jnp.clip(1.0 + 0.18 * jax.random.normal(key_of[8], (INNER,), jnp.float32), 0.1, 1.9)
    w_out = bell_draw(key_of[9], (INNER, D), INNER ** -0.5, 0.125, ((0, 2),))
    cotangent = bell_draw(key_of[10], (TOTAL, D), 1.0, 6.0, ((0, 16),))
    return dict(hidden=hidden, ids=ids, w_value=w_value, w_bc=w_bc, w_step=w_step, step_bias=step_bias, decay_log=decay_log, skip=skip, norm_gain=norm_gain, w_out=w_out, cotangent=cotangent)


precise = lax.Precision.HIGHEST
epsilon = 1e-05

def block_pieces(values, b_matrix, c_matrix, step_size, log_decay, skip_vec):
    length, head_count, _ = values.shape
    groups = b_matrix.shape[1]
    per_group = head_count // groups
    cumulative = jnp.cumsum(log_decay, axis=0)
    cum_heads = cumulative.T
    spread_log = cum_heads[:, :, None] - cum_heads[:, None, :]
    row_index = lax.broadcasted_iota(jnp.int32, (length, length), 0)
    col_index = lax.broadcasted_iota(jnp.int32, (length, length), 1)
    decay_matrix = jnp.exp(jnp.where((row_index >= col_index)[None], spread_log, -1e+30))
    scores = jnp.einsum('tgn,sgn->gts', c_matrix, b_matrix, precision=precise)
    weights = (decay_matrix.reshape(groups, per_group, length, length) * scores[:, None]).reshape(head_count, length, length)
    scaled = values * step_size[:, :, None]
    local_out = jnp.einsum('hts,shp->thp', weights, scaled, precision=precise) + skip_vec[None, :, None] * values
    tail_decay = jnp.exp(cumulative[-1][None, :] - cumulative)
    b_heads = jnp.repeat(b_matrix, per_group, axis=1)
    end_state = jnp.einsum('sh,shp,shn->hpn', tail_decay, scaled, b_heads, precision=precise)
    return (local_out, cumulative, jnp.exp(cumulative[-1]), end_state)

def carry_term(c_matrix, cumulative, start_state):
    per_group = start_state.shape[0] // c_matrix.shape[1]
    c_heads = jnp.repeat(c_matrix, per_group, axis=1)
    return jnp.einsum('thn,hpn->thp', c_heads, start_state, precision=precise) * jnp.exp(cumulative)[:, :, None]

def group_norm(mixed_out, gain_vec, groups):
    length = mixed_out.shape[0]
    grouped = mixed_out.reshape(length, groups, -1)
    scale = lax.rsqrt(lax.optimization_barrier(jnp.mean(grouped * grouped, axis=2, keepdims=True)) + epsilon)
    return (grouped * scale).reshape(length, -1) * gain_vec[None, :]

def project(source, w_value, w_bc, w_step, head_count):
    length = source.shape[0]
    values = jnp.dot(source, w_value, preferred_element_type=jnp.float32).astype(jnp.bfloat16)
    groups = w_bc.shape[1]
    state_width = w_bc.shape[2] // 2
    mixed = jnp.dot(source, w_bc.reshape(w_bc.shape[0], -1), preferred_element_type=jnp.float32).astype(jnp.bfloat16)
    mixed = mixed.reshape(length, groups, 2 * state_width).astype(jnp.float32)
    step_raw = jnp.dot(source, w_step, preferred_element_type=jnp.float32)
    return (values.astype(jnp.float32).reshape(length, head_count, -1), mixed[:, :, :state_width], mixed[:, :, state_width:], step_raw)

def direction_run(inputs, consts, flipped):
    values, b_matrix, c_matrix, step_raw = inputs
    step_bias, decay_log, skip_vec, gain_vec = consts
    if flipped:
        values, b_matrix, c_matrix, step_raw = (values[::-1], b_matrix[::-1], c_matrix[::-1], step_raw[::-1])
    step_size = jax.nn.softplus(step_raw + step_bias[None, :])
    log_decay = -jnp.exp(decay_log)[None, :] * step_size
    count = values.shape[0] // L_DEV
    head_count = values.shape[1]

    def advance(state, block):
        vals, b_blk, c_blk, s_blk, l_blk = block
        local_out, cumulative, total_decay, end_state = block_pieces(vals, b_blk, c_blk, s_blk, l_blk, skip_vec)
        mixed_out = local_out + carry_term(c_blk, cumulative, state)
        return (total_decay[:, None, None] * state + end_state, group_norm(mixed_out, gain_vec, GROUPS))
    blocks = tuple((array.reshape((count, L_DEV) + array.shape[1:]) for array in (values, b_matrix, c_matrix, step_size, log_decay)))
    initial = jnp.zeros((head_count, HEAD_DIM, STATE), jnp.float32)
    _, normed = lax.scan(jax.checkpoint(advance), initial, blocks)
    normed = normed.reshape(values.shape[0], -1)
    if flipped:
        normed = normed[::-1]
    return normed

def times_transposed(left, right):
    return lax.dot_general(left, right, (((1,), (1,)), ((), ())), preferred_element_type=jnp.float32)

def input_terms(packed, w_value, w_bc, w_step):
    inner_width = w_value.shape[1]
    bc_width = w_bc.shape[1] * w_bc.shape[2]
    total_terms = times_transposed(packed[:, :inner_width], w_value)
    total_terms = total_terms + times_transposed(packed[:, inner_width:inner_width + bc_width], w_bc.reshape(w_bc.shape[0], -1))
    return total_terms + times_transposed(packed[:, inner_width + bc_width:], w_step)

def pack_grads(first, second):
    length = first[0].shape[0]
    d_values = (first[0] + second[0]).reshape(length, -1)
    d_bc = jnp.concatenate([first[1] + second[1], first[2] + second[2]], axis=2).reshape(length, -1)
    d_step = first[3] + second[3]
    return jnp.concatenate([d_values, d_bc, d_step], axis=1).astype(jnp.bfloat16)

def reference(hidden, ids, w_value, w_bc, w_step, step_bias, decay_log, skip, norm_gain, w_out, cotangent):
    consts = (step_bias, decay_log, skip, norm_gain)
    normed = []
    local_back = []
    for source in (hidden, hidden[:, ::-1]):
        inputs = project(source, w_value, w_bc, w_step, HEADS)
        for flipped in (False, True):
            result, back = jax.vjp(partial(direction_run, consts=consts, flipped=flipped), inputs)
            normed.append(result)
            local_back.append(back)
    z_main = (normed[0] + normed[1]).astype(jnp.bfloat16)
    z_rc = (normed[2] + normed[3]).astype(jnp.bfloat16)
    out_terms = jnp.dot(z_main, w_out, preferred_element_type=jnp.float32) + jnp.dot(z_rc, w_out, preferred_element_type=jnp.float32)[:, ::-1]
    out = out_terms.astype(jnp.bfloat16)
    known_base = (ids != 4).astype(jnp.bfloat16)[:, None]
    grad = cotangent * known_base
    dz_main = times_transposed(grad, w_out).astype(jnp.bfloat16).astype(jnp.float32)
    dz_rc = times_transposed(grad[:, ::-1], w_out).astype(jnp.bfloat16).astype(jnp.float32)
    grads = [local_back[0](dz_main)[0], local_back[1](dz_main)[0], local_back[2](dz_rc)[0], local_back[3](dz_rc)[0]]
    packed_main = pack_grads(grads[0], grads[1])
    packed_rc = pack_grads(grads[2], grads[3])
    terms = input_terms(packed_main, w_value, w_bc, w_step) + input_terms(packed_rc, w_value, w_bc, w_step)[:, ::-1]
    return (out, terms.astype(jnp.bfloat16))
```

```python
from functools import partial

import jax
import jax.numpy as jnp
from jax import lax
from jax.experimental import pallas as pl
from jax.experimental.pallas import tpu as pltpu
from jax.sharding import PartitionSpec as P

f32, bf16 = jnp.float32, jnp.bfloat16
epsilon = 1e-05
LANES = 128
CHUNK = 256
NN = (((1,), (0,)), ((), ()))
NT = (((1,), (1,)), ((), ()))
TN = (((0,), (0,)), ((), ()))
MESH_ID = pl.DeviceIdType.MESH
COLUMNS = ("cum", "exc", "low", "high", "grow_f", "grow_r", "tail_f", "tail_r")

NAMES = (
    "hidden_hbm", "cot_hbm", "wv_hbm", "wo_hbm", "ids", "step_t", "bc_t", "bias", "decay", "skip",
    "gain", "out", "dh", "src", "grd", "wv", "wo", "side", "x", "dz", "y", "z", "dy", "dx", "tail",
    "aux", "cols", "rows", "bc", "scores", "dscore", "bct", "keep", "end_row", "dec_row", "dec_got",
    "dec", "par", "got", "back", "fin", "out_snd", "out_rcv", "dh_snd", "dh_rcv", "load_sem",
    "dec_sem", "go_sem", "home_sem", "mp_sem", "barrier",
)

def dot(a, b, dims=NN):
    return lax.dot_general(a, b, dims, preferred_element_type=f32)


def iota2(shape, axis):
    return lax.broadcasted_iota(jnp.int32, shape, axis)


def mirror_matrix():
    return (iota2((CHUNK, CHUNK), 0) + iota2((CHUNK, CHUNK), 1) == CHUNK - 1).astype(bf16)


def chunk_at(start):
    return pl.ds(pl.multiple_of(start, CHUNK), CHUNK)


def lanes_of(h):
    return pl.ds(h * LANES, LANES)


def exact_dot(matrix, value, used):
    hi = value.astype(bf16).astype(f32)
    rest = value - hi
    mid = rest.astype(bf16).astype(f32)
    low = (rest - mid).astype(bf16).astype(f32)
    packed = hi + pltpu.roll(mid, used, 1) + pltpu.roll(low, 2 * used, 1)
    result = dot(matrix, packed.astype(bf16))
    result += pltpu.roll(result, LANES - used, 1) + pltpu.roll(result, LANES - 2 * used, 1)
    return jnp.where(iota2(value.shape, 1) < used, result, 0.0)


class Layer:
    def __init__(self, sizes, refs):
        self.length, self.width, self.inner, self.heads, self.state, self.count, self.parts = sizes
        for name, ref in zip(NAMES, refs):
            setattr(self, name, ref)
        self.me = lax.axis_index("seq")
        self.mine = lax.axis_index("mp")
        self.share = self.width // self.parts
        self.chunks = self.share // CHUNK

    def loads(self):
        top = self.src.at[pl.ds(0, self.length)]
        bottom = self.grd.at[pl.ds(0, self.length)]
        pairs = [(self.hidden_hbm, top), (self.wv_hbm, self.wv), (self.cot_hbm, bottom), (self.wo_hbm, self.wo)]
        return [pltpu.make_async_copy(a, b, self.load_sem.at[i]) for i, (a, b) in enumerate(pairs)]

    def peer(self, hop):
        return lax.rem(self.me + hop, self.count)

    def mp_peer(self, hop):
        return lax.rem(self.mine + hop, self.parts)

    def greet(self):
        def one(hop, none):
            pl.semaphore_signal(self.barrier, inc=1, device_id={"seq": self.peer(hop)}, device_id_type=MESH_ID)
            return none

        lax.fori_loop(1, self.count, one, 0)
        for hop in range(1, self.parts):
            pl.semaphore_signal(self.barrier, inc=1, device_id={"mp": self.mp_peer(hop)}, device_id_type=MESH_ID)

    def meet(self):
        pl.semaphore_wait(self.barrier, self.count + self.parts - 2)

    def decay_copy(self, hop):
        return pltpu.make_async_remote_copy(
            src_ref=self.dec_row, dst_ref=self.dec_got.at[self.me],
            send_sem=self.dec_sem.at[0, hop], recv_sem=self.dec_sem.at[1, hop],
            device_id={"seq": self.peer(hop)}, device_id_type=MESH_ID,
        )

    def go_copy(self, e, s, hop):
        k = 2 * e + s
        return pltpu.make_async_remote_copy(
            src_ref=self.par.at[e, s, self.peer(hop)], dst_ref=self.got.at[e, s, self.me],
            send_sem=self.go_sem.at[0, k, hop], recv_sem=self.go_sem.at[1, k, hop],
            device_id={"seq": self.peer(hop)}, device_id_type=MESH_ID,
        )

    def home_copy(self, e, s, hop):
        k = 2 * e + s
        return pltpu.make_async_remote_copy(
            src_ref=self.back.at[e, s, self.peer(hop)], dst_ref=self.fin.at[e, s, self.me],
            send_sem=self.home_sem.at[0, k, hop], recv_sem=self.home_sem.at[1, k, hop],
            device_id={"seq": self.peer(hop)}, device_id_type=MESH_ID,
        )

    def mp_copy(self, which, hop, k):
        snd, rcv = (self.out_snd, self.out_rcv) if which == 0 else (self.dh_snd, self.dh_rcv)
        return pltpu.make_async_remote_copy(
            src_ref=snd.at[hop - 1, k], dst_ref=rcv.at[hop - 1, k],
            send_sem=self.mp_sem.at[0, which, hop - 1, k], recv_sem=self.mp_sem.at[1, which, hop - 1, k],
            device_id={"mp": self.mp_peer(hop)}, device_id_type=MESH_ID,
        )

    def start(self, copy, *where):
        def one(hop, none):
            copy(*where, hop).start()
            return none

        lax.fori_loop(1, self.count, one, 0)

    def finish(self, copy, *where):
        def one(hop, none):
            copy(*where, hop).wait()
            return none

        lax.fori_loop(1, self.count, one, 0)

    def put_rows(self, ref, e, s, h, which, value):
        per, rows = self.count // self.heads, ref.shape[4]
        for k in range(per):
            ref[e, s, h * per + k, which] = value[k * rows : (k + 1) * rows].astype(bf16)

    def take_rows(self, ref, e, s, h, which):
        per = self.count // self.heads
        return jnp.concatenate([ref[e, s, h * per + k, which].astype(f32) for k in range(per)], axis=0)

    def scan(self, e, s):
        count, rows = self.count, self.got.shape[4]
        self.got[e, s, self.me] = self.par[e, s, self.me]
        zero = jnp.zeros((rows, LANES), f32)

        def step(i, totals):
            result = []
            for which in range(2):
                j = i if which == e else count - 1 - i
                self.back[e, s, j, which] = totals[which].astype(bf16)
                result.append(self.dec[s, pl.ds(j, 1)] * totals[which] + self.got[e, s, j, which].astype(f32))
            return tuple(result)

        lax.fori_loop(0, count, step, (zero, zero))

    def own_decays(self):
        count, heads = self.count, self.heads
        self.dec_got[self.me] = self.dec_row[...]
        table = jnp.concatenate([self.dec_got[j] for j in range(count)], axis=0)
        lane = iota2((count, LANES), 1)
        head = self.me // (count // heads)
        for s in range(2):
            picked = jnp.sum(jnp.where(lane == s * heads + head, table, 0.0), axis=1, keepdims=True)
            self.dec[s] = jnp.broadcast_to(picked, (count, LANES))

    def flip_into(self, ref):
        mirror = mirror_matrix()

        def one(k, none):
            tile = ref[pl.ds(0, self.length), chunk_at(k * CHUNK)]
            ref[pl.ds(self.length, self.length), chunk_at(self.width - CHUNK - k * CHUNK)] = dot(tile, mirror).astype(bf16)
            return none

        lax.fori_loop(0, self.width // CHUNK, one, 0)

    def side_weights(self):
        gap = LANES - self.heads - 2 * self.state
        self.side[...] = jnp.concatenate(
            [self.step_t[...].astype(f32), jnp.zeros((gap, self.width), f32), self.bc_t[...].astype(f32)], axis=0
        ).astype(bf16)

    def prepare(self):
        length, heads, state, used = self.length, self.heads, self.state, 2 * self.heads
        shape = (length, LANES)
        lane = iota2(shape, 1)
        aux = dot(self.src[...], self.side[...], NT)
        self.aux[0], self.aux[1] = aux[:length], aux[length:]
        raw = jnp.where(lane < heads, aux[:length], pltpu.roll(aux[length:], heads, 1))
        spare = jnp.zeros((1, LANES - used), f32)
        bias = jnp.concatenate([self.bias[...], self.bias[...], spare], axis=1)
        rate = jnp.exp(jnp.concatenate([self.decay[...], self.decay[...], spare], axis=1))
        shifted = jnp.where(lane < used, raw + bias, 0.0)
        dt = jnp.maximum(shifted, 0.0) + jnp.log1p(jnp.exp(-jnp.abs(shifted)))
        la = jnp.where(lane < used, -rate * dt, 0.0)
        lower = (iota2((length, length), 0) >= iota2((length, length), 1)).astype(bf16)
        cum = exact_dot(lower, la, used)
        exc = cum - la
        end = cum[length - 1 : length]
        log_dt = jnp.log(jnp.maximum(dt, 1e-38))
        grow_f, grow_r = jnp.exp(cum), jnp.exp(end - exc)
        tail_f, tail_r = dt * jnp.exp(end - cum), dt * jnp.exp(exc)
        values = (cum, exc, cum - log_dt, exc + log_dt, grow_f, grow_r, tail_f, tail_r)
        for i, value in enumerate(values):
            self.cols[i, 0] = value
            self.cols[i, 1] = pltpu.roll(value, LANES - heads, 1)
            flat = value.T
            self.rows[i, 0], self.rows[i, 1] = flat[:heads], flat[heads:used]
        sig = jax.nn.sigmoid(shifted)
        ratio = jnp.where(shifted < -15.0, 1.0, sig / jnp.maximum(dt, 1e-38))
        for i, value in ((0, sig * rate), (1, ratio)):
            self.keep[i, 0] = value
            self.keep[i, 1] = pltpu.roll(value, LANES - heads, 1)
        self.dec_row[...] = jnp.exp(end)
        for s in range(2):
            rounded = self.aux[s].astype(bf16)
            b_m, c_m = rounded[:, LANES - 2 * state : LANES - state], rounded[:, LANES - state :]
            self.bc[s, 0, :, :state] = b_m
            self.bc[s, 1, :, :state] = c_m
            self.bct[s] = rounded.astype(f32).T[LANES - 2 * state :]

    def row(self, name, s, h):
        return self.rows[COLUMNS.index(name), s, pl.ds(h, 1)]

    def col(self, name, s, h, at):
        return self.cols[COLUMNS.index(name), s, at, h : h + 1]

    def ends(self, s):
        b_t = self.bct[s, : self.state]
        for h in range(self.heads):
            left = jnp.concatenate([b_t * self.row("tail_f", s, h), b_t * self.row("tail_r", s, h)], axis=0).astype(bf16)
            both = dot(left, self.x[s, :, lanes_of(h)])
            self.put_rows(self.par, 0, s, h, 0, both[: self.state])
            self.put_rows(self.par, 0, s, h, 1, both[self.state :])

    def blocks(self):
        return [pl.ds(k * LANES, LANES) for k in range(self.length // LANES)]

    def local_outputs(self, s):
        at, state = self.blocks(), self.state
        b_m, c_m = self.bc[s, 0, :, :state], self.bc[s, 1, :, :state]
        self.scores[...] = dot(c_m, b_m, NT)
        below = iota2((LANES, LANES), 0) - iota2((LANES, LANES), 1)
        none = jnp.zeros((LANES, LANES), bf16)
        for h in range(self.heads):
            low_rows, high_rows = [], []
            for i, t in enumerate(at):
                cum, exc = self.col("cum", s, h, t), self.col("exc", s, h, t)
                low_cols, high_cols = [], []
                for j in range(len(at)):
                    cut = slice(j * LANES, (j + 1) * LANES)
                    to_f = lambda: cum - self.row("low", s, h)[:, cut]
                    to_r = lambda: self.row("high", s, h)[:, cut] - exc
                    power = to_f() if i > j else to_r() if i < j else jnp.minimum(to_f(), to_r())
                    mix = jnp.exp(power) * self.scores[t, cut]
                    low_cols.append(none if i < j else mix.astype(bf16) if i > j else jnp.where(below >= 0, mix, 0.0).astype(bf16))
                    high_cols.append(none if i > j else mix.astype(bf16) if i < j else jnp.where(below <= 0, mix, 0.0).astype(bf16))
                low_rows.append(jnp.concatenate(low_cols, axis=1))
                high_rows.append(jnp.concatenate(high_cols, axis=1))
            both = dot(jnp.concatenate(low_rows + high_rows, axis=0), self.x[s, :, lanes_of(h)])
            self.y[s, 0, :, lanes_of(h)] = both[: self.length]
            self.y[s, 1, :, lanes_of(h)] = both[self.length :]

    def finish_outputs(self, s):
        length, heads, state = self.length, self.heads, self.state
        at = self.blocks()
        c_m = self.bc[s, 1, :, :state]
        c_t = self.bct[s, state:]
        squares = [[jnp.zeros((LANES, LANES), f32) for _ in at] for _ in range(2)]
        for h in range(heads):
            for d, grow in ((0, "grow_f"), (1, "grow_r")):
                carried = dot(c_m, self.take_rows(self.fin, 0, s, h, d).astype(bf16))
                for i, t in enumerate(at):
                    y = self.y[s, d, t, lanes_of(h)] + self.col(grow, s, h, t) * carried[i * LANES : (i + 1) * LANES]
                    self.y[s, d, t, lanes_of(h)] = y
                    y += self.skip[:, h : h + 1] * self.x[s, t, lanes_of(h)].astype(f32)
                    squares[d][i] += y * y
        share = 1.0 / (heads * LANES)
        scale = [
            [lax.rsqrt(jnp.sum(q, axis=1, keepdims=True) * share + epsilon) for q in of_direction]
            for of_direction in squares
        ]
        means = []
        for i, t in enumerate(at):
            m_f, m_r = jnp.zeros((LANES, LANES), f32), jnp.zeros((LANES, LANES), f32)
            for h in range(heads):
                gain = self.gain[:, lanes_of(h)]
                direct = self.skip[:, h : h + 1] * self.x[s, t, lanes_of(h)].astype(f32)
                n_f = (self.y[s, 0, t, lanes_of(h)] + direct) * scale[0][i]
                n_r = (self.y[s, 1, t, lanes_of(h)] + direct) * scale[1][i]
                self.z[s, t, lanes_of(h)] = ((n_f + n_r) * gain).astype(bf16)
                g = self.dz[s, t, lanes_of(h)].astype(f32) * gain
                m_f += g * n_f
                m_r += g * n_r
            means.append([jnp.sum(m, axis=1, keepdims=True) * share for m in (m_f, m_r)])
        lane = iota2((LANES, LANES), 1)
        for i, t in enumerate(at):
            given = [jnp.zeros((LANES, LANES), f32) for _ in range(2)]
            pull = [scale[d][i] * scale[d][i] * means[i][d] for d in range(2)]
            for h in range(heads):
                g = self.dz[s, t, lanes_of(h)].astype(f32) * self.gain[:, lanes_of(h)]
                direct = self.skip[:, h : h + 1] * self.x[s, t, lanes_of(h)].astype(f32)
                for d in range(2):
                    y = self.y[s, d, t, lanes_of(h)]
                    grad = (scale[d][i] * g - pull[d] * (y + direct)).astype(bf16)
                    self.dy[s, d, t, lanes_of(h)] = grad
                    total = jnp.sum(grad.astype(f32) * y, axis=1, keepdims=True)
                    given[d] = jnp.where(lane == h, total, given[d])
            for d in range(2):
                self.cols[d, s, t] = given[d]
        for h in range(heads):
            for d, grow in ((0, "grow_f"), (1, "grow_r")):
                left = (c_t * self.row(grow, s, h)).astype(bf16)
                self.put_rows(self.par, 1, s, h, d, dot(left, self.dy[s, d, :, lanes_of(h)]))

    def local_grads(self, s):
        at, state = self.blocks(), self.state
        b_m, c_m = self.bc[s, 0, :, :state], self.bc[s, 1, :, :state]
        self.scores[...] = dot(b_m, c_m, NT)
        self.dscore[s] = jnp.zeros_like(self.scores)
        above = iota2((LANES, LANES), 1) - iota2((LANES, LANES), 0)
        none = jnp.zeros((LANES, LANES), bf16)
        for h in range(self.heads):
            x_h = self.x[s, :, lanes_of(h)]
            d_f, d_r = self.dy[s, 0, :, lanes_of(h)], self.dy[s, 1, :, lanes_of(h)]
            p_f, p_r = dot(x_h, d_f, NT), dot(x_h, d_r, NT)
            f_rows, r_rows = [], []
            for i, t in enumerate(at):
                low, high = self.col("low", s, h, t), self.col("high", s, h, t)
                f_cols, r_cols = [], []
                for j in range(len(at)):
                    here = slice(i * LANES, (i + 1) * LANES), slice(j * LANES, (j + 1) * LANES)
                    to_f = lambda: self.row("cum", s, h)[:, here[1]] - low
                    to_r = lambda: high - self.row("exc", s, h)[:, here[1]]
                    power = to_f() if i < j else to_r() if i > j else jnp.minimum(to_f(), to_r())
                    decay = jnp.exp(power)
                    weight = decay * self.scores[here]
                    if i < j:
                        picked = p_f[here]
                        f_cols.append(weight.astype(bf16))
                        r_cols.append(none)
                    elif i > j:
                        picked = p_r[here]
                        f_cols.append(none)
                        r_cols.append(weight.astype(bf16))
                    else:
                        picked = jnp.where(above >= 0, p_f[here], 0.0) + jnp.where(above <= 0, p_r[here], 0.0)
                        f_cols.append(jnp.where(above >= 0, weight, 0.0).astype(bf16))
                        r_cols.append(jnp.where(above <= 0, weight, 0.0).astype(bf16))
                    self.dscore[s, t, here[1]] += decay * picked
                f_rows.append(jnp.concatenate(f_cols, axis=1))
                r_rows.append(jnp.concatenate(r_cols, axis=1))
            self.y[s, 0, :, lanes_of(h)] = dot(jnp.concatenate(f_rows, axis=0), d_f)
            self.y[s, 1, :, lanes_of(h)] = dot(jnp.concatenate(r_rows, axis=0), d_r)

    def finish_grads(self, s):
        length, heads, state = self.length, self.heads, self.state
        at = self.blocks()
        b_m, c_m = self.bc[s, 0, :, :state], self.bc[s, 1, :, :state]
        lane = iota2((LANES, LANES), 1)
        lane_row = iota2((1, LANES), 1)
        zero = jnp.zeros((LANES, LANES), f32)
        into = [[zero for _ in at] for _ in range(2)]
        total = jnp.zeros((1, LANES), f32)
        d_b = jnp.zeros((length, state), f32)
        d_c = jnp.zeros((length, state), f32)
        ends = jnp.exp(self.end_row[s])
        for h in range(heads):
            x_h = self.x[s, :, lanes_of(h)]
            s_f, s_r = self.take_rows(self.fin, 0, s, h, 0), self.take_rows(self.fin, 0, s, h, 1)
            a_f, a_r = self.take_rows(self.fin, 1, s, h, 0), self.take_rows(self.fin, 1, s, h, 1)
            own, own_r = self.take_rows(self.par, 0, s, h, 0), self.take_rows(self.par, 1, s, h, 1)
            whole = pl.ds(0, length)
            tail_f, tail_r = self.col("tail_f", s, h, whole), self.col("tail_r", s, h, whole)
            u_f, u_r = dot(b_m, a_f.astype(bf16)), dot(b_m, a_r.astype(bf16))
            d_b += dot(x_h, a_f.astype(bf16), NT) * tail_f + dot(x_h, a_r.astype(bf16), NT) * tail_r
            d_c += dot(self.dy[s, 0, :, lanes_of(h)], s_f.astype(bf16), NT) * self.col("grow_f", s, h, whole)
            d_c += dot(self.dy[s, 1, :, lanes_of(h)], s_r.astype(bf16), NT) * self.col("grow_r", s, h, whole)
            for i, t in enumerate(at):
                cut = slice(i * LANES, (i + 1) * LANES)
                x = self.x[s, t, lanes_of(h)].astype(f32)
                u = [
                    self.y[s, 0, t, lanes_of(h)] + tail_f[cut] * u_f[cut],
                    self.y[s, 1, t, lanes_of(h)] + tail_r[cut] * u_r[cut],
                ]
                skipped = self.dy[s, 0, t, lanes_of(h)].astype(f32) + self.dy[s, 1, t, lanes_of(h)].astype(f32)
                self.dx[s, t, lanes_of(h)] = (u[0] + u[1] + self.skip[:, h : h + 1] * skipped).astype(bf16)
                for d in range(2):
                    into[d][i] = jnp.where(lane == h, jnp.sum(x * u[d], axis=1, keepdims=True), into[d][i])
            decay = ends[:, h : h + 1]
            ending = a_f * (decay * s_f + own) + s_r * (decay * a_r + own_r)
            ended = jnp.sum(jnp.sum(ending, axis=0, keepdims=True), axis=1, keepdims=True)
            total = jnp.where(lane_row == h, ended, total)
        into_f, into_r = (jnp.concatenate(rows, axis=0) for rows in into)
        d_cum = self.cols[0, s] - into_f
        d_exc = into_r - self.cols[1, s]
        upper = (iota2((length, length), 0) <= iota2((length, length), 1)).astype(bf16)
        d_la = exact_dot(upper, d_cum + d_exc, heads) - d_exc + total
        d_raw = (into_f + into_r) * self.keep[1, s] - self.keep[0, s] * d_la
        d_raw = jnp.where(iota2((length, LANES), 1) < heads, d_raw, 0.0)
        scores = self.dscore[s].astype(bf16)
        d_b += dot(scores, c_m)
        d_c += dot(scores, b_m, TN)
        self.tail[s] = jnp.concatenate([d_raw[:, : LANES - 2 * state], d_b, d_c], axis=1).astype(bf16)

    def out_chunk(self, part, k):
        first = part * self.share + k * CHUNK
        there = self.width - CHUNK - first
        mirrored = dot(self.z[1], self.wo[:, chunk_at(there)]).astype(bf16)
        return dot(self.z[0], self.wo[:, chunk_at(first)]) + dot(mirrored, mirror_matrix())

    def hidden_chunk(self, part, k):
        first = part * self.share + k * CHUNK
        there = self.width - CHUNK - first

        def term(s, at):
            return dot(self.dx[s], self.wv[chunk_at(at), :], NT) + dot(self.tail[s], self.side[:, chunk_at(at)])

        return term(0, first) + dot(term(1, there).astype(bf16), mirror_matrix())

    def send_parts(self, which, chunk):
        snd = self.out_snd if which == 0 else self.dh_snd
        for hop in range(1, self.parts):

            def one(k, none, hop=hop):
                snd[hop - 1, k] = chunk(self.mp_peer(hop), k).astype(bf16)
                self.mp_copy(which, hop, k).start()
                return none

            lax.fori_loop(0, self.chunks, one, 0)

    def own_part(self, which, chunk):
        rcv, out = (self.out_rcv, self.out) if which == 0 else (self.dh_rcv, self.dh)

        def one(k, none):
            value = chunk(self.mine, k)
            for hop in range(1, self.parts):
                self.mp_copy(which, hop, k).wait()
                value += rcv[hop - 1, k].astype(f32)
            out[:, chunk_at(k * CHUNK)] = value.astype(bf16)
            return none

        lax.fori_loop(0, self.chunks, one, 0)


def each_stream(body):
    def one(s, none):
        body(s)
        return none

    lax.fori_loop(0, 2, one, 0)


def layer_kernel(sizes, *refs):
    layer = Layer(sizes, refs + (pltpu.get_barrier_semaphore(),))
    length, inner = layer.length, layer.inner
    hidden_load, value_load, cot_load, out_load = layer.loads()
    for load in (hidden_load, value_load, cot_load, out_load):
        load.start()
    layer.greet()
    layer.side_weights()
    hidden_load.wait()
    layer.flip_into(layer.src)
    layer.prepare()
    for s in range(2):
        layer.end_row[s] = layer.cols[0, s, length - 1 : length]
    layer.meet()
    layer.start(layer.decay_copy)
    value_load.wait()

    def values(k, none):
        at = chunk_at(k * CHUNK)
        both = dot(layer.src[...], layer.wv[:, at]).astype(bf16)
        layer.x[0, :, at], layer.x[1, :, at] = both[:length], both[length:]
        return none

    lax.fori_loop(0, inner // CHUNK, values, 0)

    def leave(s):
        layer.ends(s)
        layer.start(layer.go_copy, 0, s)

    each_stream(leave)
    cot_load.wait()
    layer.flip_into(layer.grd)
    known = jnp.where(layer.ids[...] != 4, 1.0, 0.0)
    known = jnp.broadcast_to(known, (8, length)).T[:, :1] > 0.5
    out_load.wait()

    def output_grads(k, none):
        at = chunk_at(k * CHUNK)
        both = dot(layer.grd[...], layer.wo[at, :], NT)
        layer.dz[0, :, at] = jnp.where(known, both[:length], 0.0).astype(bf16)
        layer.dz[1, :, at] = jnp.where(known, both[length:], 0.0).astype(bf16)
        return none

    lax.fori_loop(0, inner // CHUNK, output_grads, 0)
    layer.finish(layer.decay_copy)
    layer.own_decays()

    def turn(e, work, s):
        layer.finish(layer.go_copy, e, s)
        layer.scan(e, s)
        layer.start(layer.home_copy, e, s)
        work(s)

    def arrive(e, s):
        layer.finish(layer.home_copy, e, s)
        layer.fin[e, s, layer.me] = layer.back[e, s, layer.me]

    each_stream(partial(turn, 0, layer.local_outputs))

    def outputs(s):
        arrive(0, s)
        layer.finish_outputs(s)
        layer.start(layer.go_copy, 1, s)

    each_stream(outputs)
    layer.send_parts(0, layer.out_chunk)
    each_stream(partial(turn, 1, layer.local_grads))

    def gradients(s):
        arrive(1, s)
        layer.finish_grads(s)

    each_stream(gradients)
    layer.send_parts(1, layer.hidden_chunk)
    layer.own_part(0, layer.out_chunk)
    layer.own_part(1, layer.hidden_chunk)


def per_device(
    hidden, ids, w_value, w_bc, w_step, step_bias, decay_log, skip, norm_gain, w_out, cotangent
):
    length, width = hidden.shape
    heads, inner, state = w_step.shape[1], w_value.shape[1], w_bc.shape[2] // 2
    count, parts = lax.axis_size("seq"), lax.axis_size("mp")
    assert w_bc.shape[1] == 1 and inner == heads * LANES
    assert count % heads == 0 and (heads * state) % count == 0
    rows = heads * state // count
    share = width // parts
    chunks = share // CHUNK
    vmem, anywhere = pl.BlockSpec(memory_space=pltpu.VMEM), pl.BlockSpec(memory_space=pl.ANY)
    parcel = (2, 2, count, 2, rows, LANES)
    travel = (max(parts - 1, 1), chunks, length, CHUNK)
    sem = pltpu.SemaphoreType.DMA
    scratch = [
        pltpu.VMEM((2 * length, width), bf16),
        pltpu.VMEM((2 * length, width), bf16),
        pltpu.VMEM(w_value.shape, bf16),
        pltpu.VMEM(w_out.shape, bf16),
        pltpu.VMEM((LANES, width), bf16),
        pltpu.VMEM((2, length, inner), bf16),
        pltpu.VMEM((2, length, inner), bf16),
        pltpu.VMEM((2, 2, length, inner), f32),
        pltpu.VMEM((2, length, inner), bf16),
        pltpu.VMEM((2, 2, length, inner), bf16),
        pltpu.VMEM((2, length, inner), bf16),
        pltpu.VMEM((2, length, LANES), bf16),
        pltpu.VMEM((2, length, LANES), f32),
        pltpu.VMEM((len(COLUMNS), 2, length, LANES), f32),
        pltpu.VMEM((len(COLUMNS), 2, heads, length), f32),
        pltpu.VMEM((2, 2, length, LANES), bf16),
        pltpu.VMEM((length, length), f32),
        pltpu.VMEM((2, length, length), f32),
        pltpu.VMEM((2, 2 * state, length), f32),
        pltpu.VMEM((2, 2, length, LANES), f32),
        pltpu.VMEM((2, 1, LANES), f32),
        pltpu.VMEM((1, LANES), f32),
        pltpu.VMEM((count, 1, LANES), f32),
        pltpu.VMEM((2, count, LANES), f32),
        pltpu.VMEM(parcel, bf16),
        pltpu.VMEM(parcel, bf16),
        pltpu.VMEM(parcel, bf16),
        pltpu.VMEM(parcel, bf16),
        pltpu.VMEM(travel, bf16),
        pltpu.VMEM(travel, bf16),
        pltpu.VMEM(travel, bf16),
        pltpu.VMEM(travel, bf16),
        sem((4,)),
        sem((2, count)),
        sem((2, 4, count)),
        sem((2, 4, count)),
        sem((2, 2, max(parts - 1, 1), chunks)),
    ]
    sizes = (length, width, inner, heads, state, count, parts)
    return pl.pallas_call(
        partial(layer_kernel, sizes),
        in_specs=[anywhere] * 4 + [vmem] * 7,
        out_specs=(vmem, vmem),
        out_shape=(jax.ShapeDtypeStruct((length, share), bf16),) * 2,
        scratch_shapes=scratch,
        compiler_params=pltpu.CompilerParams(
            collective_id=0, has_side_effects=True, vmem_limit_bytes=56 * 1024 * 1024
        ),
    )(
        hidden, cotangent, w_value, w_out, ids[None], w_step.T, w_bc.reshape(width, -1).T,
        step_bias[None], decay_log[None], skip[None], norm_gain[None],
    )


def solution(mesh):
    in_specs = (
        P("seq", None),
        P("seq"),
        P(None, "mp"),
        P(None, "mp", None),
        P(None, "mp"),
        P("mp"),
        P("mp"),
        P("mp"),
        P("mp"),
        P("mp", None),
        P("seq", None),
    )
    out_specs = (P("seq", "mp"), P("seq", "mp"))
    return jax.shard_map(
        per_device, mesh=mesh, in_specs=in_specs, out_specs=out_specs, check_vma=False
    )
```

```python
from functools import partial

import jax
import jax.numpy as jnp
from jax import lax
from jax.experimental import pallas as pl
from jax.experimental.pallas import tpu as pltpu
from jax.sharding import PartitionSpec as P

f32, bf16 = jnp.float32, jnp.bfloat16
epsilon = 1e-05
LANES = 128
CHUNK = 256
NN = (((1,), (0,)), ((), ()))
NT = (((1,), (1,)), ((), ()))
TN = (((0,), (0,)), ((), ()))
MESH_ID = pl.DeviceIdType.MESH
COLUMNS = ("cum", "exc", "low", "high", "grow_f", "grow_r", "tail_f", "tail_r")

NAMES = (
    "hidden_hbm", "cot_hbm", "wv_hbm", "wo_hbm", "ids", "step_t", "bc_t", "bias", "decay", "skip",
    "gain", "out", "dh", "src", "grd", "wv", "wo", "side", "x", "dz", "y", "z", "dy", "dx", "tail",
    "aux", "cols", "rows", "bc", "scores", "dscore", "carried", "bct", "keep", "end_row", "dec_row",
    "dec_got", "dec", "plane_dec", "par", "got", "agg", "far", "back", "fin", "out_snd", "out_rcv",
    "dh_snd", "dh_rcv", "hold", "load_sem", "dec_sem", "go_sem", "far_sem", "home_sem", "mp_sem",
    "barrier",
)


def dot(a, b, dims=NN):
    return lax.dot_general(a, b, dims, preferred_element_type=f32)


def iota2(shape, axis):
    return lax.broadcasted_iota(jnp.int32, shape, axis)


def mirror_matrix():
    return (iota2((CHUNK, CHUNK), 0) + iota2((CHUNK, CHUNK), 1) == CHUNK - 1).astype(bf16)


def chunk_at(start):
    return pl.ds(pl.multiple_of(start, CHUNK), CHUNK)


def lanes_of(h):
    return pl.ds(h * LANES, LANES)


def exact_dot(matrix, value, used):
    hi = value.astype(bf16).astype(f32)
    rest = value - hi
    mid = rest.astype(bf16).astype(f32)
    low = (rest - mid).astype(bf16).astype(f32)
    packed = hi + pltpu.roll(mid, used, 1) + pltpu.roll(low, 2 * used, 1)
    result = dot(matrix, packed.astype(bf16))
    result += pltpu.roll(result, LANES - used, 1) + pltpu.roll(result, LANES - 2 * used, 1)
    return jnp.where(iota2(value.shape, 1) < used, result, 0.0)


class Layer:
    def __init__(self, sizes, refs):
        self.length, self.width, self.inner, self.heads, self.state, self.count, self.group, self.parts = sizes
        for name, ref in zip(NAMES, refs):
            setattr(self, name, ref)
        self.planes = self.count // self.group
        self.each = self.heads // self.group
        me = lax.axis_index("seq")
        self.me, self.plane, self.member = me, me // self.group, lax.rem(me, self.group)
        self.mine = lax.axis_index("mp")
        self.share = self.width // self.parts
        self.chunks = self.share // CHUNK

    def loads(self):
        top = self.src.at[pl.ds(0, self.length)]
        bottom = self.grd.at[pl.ds(0, self.length)]
        pairs = [(self.hidden_hbm, top), (self.wv_hbm, self.wv), (self.cot_hbm, bottom), (self.wo_hbm, self.wo)]
        return [pltpu.make_async_copy(a, b, self.load_sem.at[i]) for i, (a, b) in enumerate(pairs)]

    def peer(self, hop):
        return lax.rem(self.me + hop, self.count)

    def greet(self):
        def one(hop, none):
            pl.semaphore_signal(self.barrier, inc=1, device_id={"seq": self.peer(hop)}, device_id_type=MESH_ID)
            return none

        lax.fori_loop(1, self.count, one, 0)
        pl.semaphore_signal(self.barrier, inc=1, device_id={"mp": 1 - self.mine}, device_id_type=MESH_ID)

    def meet(self):
        pl.semaphore_wait(self.barrier, self.count)

    def remote(self, src, dst, sems, where, device):
        return pltpu.make_async_remote_copy(
            src_ref=src, dst_ref=dst, send_sem=sems.at[(0,) + where], recv_sem=sems.at[(1,) + where],
            device_id=device, device_id_type=MESH_ID,
        )

    def decay_copy(self, hop):
        return self.remote(self.dec_row, self.dec_got.at[self.me], self.dec_sem, (hop,), {"seq": self.peer(hop)})

    def start_decays(self):
        def one(hop, none):
            self.decay_copy(hop).start()
            return none

        lax.fori_loop(1, self.count, one, 0)

    def finish_decays(self):
        def one(hop, none):
            self.decay_copy(hop).wait()
            return none

        lax.fori_loop(1, self.count, one, 0)

    def gather_copies(self, e, s):
        for hop in range(1, self.group):
            to = lax.rem(self.member + hop, self.group)
            yield self.remote(
                self.par.at[e, s, to], self.got.at[e, s, self.member], self.go_sem, (2 * e + s, hop),
                {"seq": self.plane * self.group + to},
            )

    def plane_copies(self, e, s):
        for hop in range(1, self.planes):
            to = lax.rem(self.plane + hop, self.planes)
            which = jnp.where(to > self.plane, e, 1 - e)
            yield self.remote(
                self.agg.at[e, s, which], self.far.at[e, s, self.plane], self.far_sem, (2 * e + s, hop),
                {"seq": to * self.group + self.member},
            )

    def home_copies(self, e, s):
        for hop in range(1, self.group):
            to = lax.rem(self.member + hop, self.group)
            yield self.remote(
                self.back.at[e, s, to], self.fin.at[e, s, self.member], self.home_sem, (2 * e + s, hop),
                {"seq": self.plane * self.group + to},
            )

    def mp_copy(self, which, k):
        snd, rcv = (self.out_snd, self.out_rcv) if which == 0 else (self.dh_snd, self.dh_rcv)
        return self.remote(snd.at[k], rcv.at[k], self.mp_sem, (which, k), {"mp": 1 - self.mine})

    def put_rows(self, e, s, h, which, value):
        at = pl.ds(h % self.each * self.state, self.state)
        self.par[e, s, h // self.each, which, at] = value.astype(bf16)

    def take_rows(self, ref, e, s, h, which):
        return ref[e, s, h // self.each, which, pl.ds(h % self.each * self.state, self.state)]

    def own_decays(self):
        self.dec_got[self.me] = self.dec_row[...]
        table = jnp.concatenate([self.dec_got[j] for j in range(self.count)], axis=0)
        lane = iota2((self.count, LANES), 1)
        for s in range(2):
            for q in range(self.each):
                head = s * self.heads + self.member * self.each + q
                picked = jnp.sum(jnp.where(lane == head, table, 0.0), axis=1, keepdims=True)
                wide = jnp.broadcast_to(picked, (self.count, LANES))
                self.dec[s, q] = wide
                for p in range(self.planes):
                    product = wide[p * self.group : p * self.group + 1]
                    for m in range(1, self.group):
                        product = product * wide[p * self.group + m : p * self.group + m + 1]
                    self.plane_dec[s, q, p : p + 1] = product

    def members(self, e, s, which, q, total, visit):
        order = range(self.group) if which == e else range(self.group - 1, -1, -1)
        at = pl.ds(q * self.state, self.state)
        for m in order:
            visit(m, at, total)
            decay = self.dec[s, q, pl.ds(self.plane * self.group + m, 1)]
            total = decay * total + self.got[e, s, m, which, at].astype(f32)
        return total

    def begin(self, e, s):
        for copy in self.gather_copies(e, s):
            copy.start()

    def spread(self, e, s):
        for copy in self.gather_copies(e, s):
            copy.wait()
        self.got[e, s, self.member] = self.par[e, s, self.member]
        self.far[e, s, self.plane] = jnp.zeros((self.each * self.state, LANES), bf16)
        for which in range(2):
            for q in range(self.each):
                total = self.members(e, s, which, q, jnp.zeros((self.state, LANES), f32), lambda m, at, total: None)
                self.agg[e, s, which, pl.ds(q * self.state, self.state)] = total.astype(bf16)
        for copy in self.plane_copies(e, s):
            copy.start()

    def send_home(self, e, s):
        for copy in self.plane_copies(e, s):
            copy.wait()
        for which in range(2):
            rising = which == e
            for q in range(self.each):
                total = jnp.zeros((self.state, LANES), f32)
                for p in range(self.planes) if rising else range(self.planes - 1, -1, -1):
                    got = self.far[e, s, p, pl.ds(q * self.state, self.state)].astype(f32)
                    longer = self.plane_dec[s, q, p : p + 1] * total + got
                    total = jnp.where(p < self.plane if rising else p > self.plane, longer, total)

                def keep(m, at, value):
                    self.back[e, s, m, which, at] = value.astype(bf16)

                self.members(e, s, which, q, total, keep)
        for copy in self.home_copies(e, s):
            copy.start()

    def arrive(self, e, s):
        for copy in self.home_copies(e, s):
            copy.wait()
        self.fin[e, s, self.member] = self.back[e, s, self.member]

    def flip_into(self, ref):
        mirror = mirror_matrix()
        for k in range(self.width // CHUNK):
            tile = ref[pl.ds(0, self.length), pl.ds(k * CHUNK, CHUNK)]
            there = pl.ds(self.width - CHUNK - k * CHUNK, CHUNK)
            ref[pl.ds(self.length, self.length), there] = dot(tile, mirror).astype(bf16)

    def side_weights(self):
        gap = LANES - self.heads - 2 * self.state
        self.side[...] = jnp.concatenate(
            [self.step_t[...].astype(f32), jnp.zeros((gap, self.width), f32), self.bc_t[...].astype(f32)], axis=0
        ).astype(bf16)

    def prepare(self):
        length, heads, state, used = self.length, self.heads, self.state, 2 * self.heads
        shape = (length, LANES)
        lane = iota2(shape, 1)
        aux = dot(self.src[...], self.side[...], NT)
        self.aux[0], self.aux[1] = aux[:length], aux[length:]
        raw = jnp.where(lane < heads, aux[:length], pltpu.roll(aux[length:], heads, 1))
        spare = jnp.zeros((1, LANES - used), f32)
        bias = jnp.concatenate([self.bias[...], self.bias[...], spare], axis=1)
        rate = jnp.exp(jnp.concatenate([self.decay[...], self.decay[...], spare], axis=1))
        shifted = jnp.where(lane < used, raw + bias, 0.0)
        dt = jnp.maximum(shifted, 0.0) + jnp.log1p(jnp.exp(-jnp.abs(shifted)))
        la = jnp.where(lane < used, -rate * dt, 0.0)
        lower = (iota2((length, length), 0) >= iota2((length, length), 1)).astype(bf16)
        cum = exact_dot(lower, la, used)
        exc = cum - la
        end = cum[length - 1 : length]
        log_dt = jnp.log(jnp.maximum(dt, 1e-38))
        grow_f, grow_r = jnp.exp(cum), jnp.exp(end - exc)
        tail_f, tail_r = dt * jnp.exp(end - cum), dt * jnp.exp(exc)
        values = (cum, exc, cum - log_dt, exc + log_dt, grow_f, grow_r, tail_f, tail_r)
        for i, value in enumerate(values):
            self.cols[i, 0] = value
            self.cols[i, 1] = pltpu.roll(value, LANES - heads, 1)
            flat = value.T
            self.rows[i, 0], self.rows[i, 1] = flat[:heads], flat[heads:used]
        sig = jax.nn.sigmoid(shifted)
        ratio = jnp.where(shifted < -15.0, 1.0, sig / jnp.maximum(dt, 1e-38))
        for i, value in ((0, sig * rate), (1, ratio)):
            self.keep[i, 0] = value
            self.keep[i, 1] = pltpu.roll(value, LANES - heads, 1)
        self.dec_row[...] = jnp.exp(end)
        for s in range(2):
            rounded = self.aux[s].astype(bf16)
            b_m, c_m = rounded[:, LANES - 2 * state : LANES - state], rounded[:, LANES - state :]
            self.bc[s, 0, :, :state] = b_m
            self.bc[s, 1, :, :state] = c_m
            self.bct[s] = rounded.astype(f32).T[LANES - 2 * state :]

    def row(self, name, s, h):
        return self.rows[COLUMNS.index(name), s, pl.ds(h, 1)]

    def col(self, name, s, h, at):
        return self.cols[COLUMNS.index(name), s, at, h : h + 1]

    def ends(self, s):
        b_t = self.bct[s, : self.state]
        for h in range(self.heads):
            left = jnp.concatenate([b_t * self.row("tail_f", s, h), b_t * self.row("tail_r", s, h)], axis=0).astype(bf16)
            both = dot(left, self.x[s, :, lanes_of(h)])
            self.put_rows(0, s, h, 0, both[: self.state])
            self.put_rows(0, s, h, 1, both[self.state :])

    def blocks(self):
        return [pl.ds(k * LANES, LANES) for k in range(self.length // LANES)]

    def local_outputs(self, s):
        at, state = self.blocks(), self.state
        b_m, c_m = self.bc[s, 0, :, :state], self.bc[s, 1, :, :state]
        self.scores[...] = dot(c_m, b_m, NT)
        below = iota2((LANES, LANES), 0) - iota2((LANES, LANES), 1)
        none = jnp.zeros((LANES, LANES), bf16)
        for h in range(self.heads):
            low_rows, high_rows = [], []
            for i, t in enumerate(at):
                cum, exc = self.col("cum", s, h, t), self.col("exc", s, h, t)
                low_cols, high_cols = [], []
                for j in range(len(at)):
                    cut = slice(j * LANES, (j + 1) * LANES)
                    to_f = lambda: cum - self.row("low", s, h)[:, cut]
                    to_r = lambda: self.row("high", s, h)[:, cut] - exc
                    power = to_f() if i > j else to_r() if i < j else jnp.minimum(to_f(), to_r())
                    mix = jnp.exp(power) * self.scores[t, cut]
                    low_cols.append(none if i < j else mix.astype(bf16) if i > j else jnp.where(below >= 0, mix, 0.0).astype(bf16))
                    high_cols.append(none if i > j else mix.astype(bf16) if i < j else jnp.where(below <= 0, mix, 0.0).astype(bf16))
                low_rows.append(jnp.concatenate(low_cols, axis=1))
                high_rows.append(jnp.concatenate(high_cols, axis=1))
            both = dot(jnp.concatenate(low_rows + high_rows, axis=0), self.x[s, :, lanes_of(h)])
            self.y[s, 0, :, lanes_of(h)] = both[: self.length]
            self.y[s, 1, :, lanes_of(h)] = both[self.length :]

    def finish_outputs(self, s):
        length, heads, state = self.length, self.heads, self.state
        at = self.blocks()
        c_m = self.bc[s, 1, :, :state]
        c_t = self.bct[s, state:]
        zero = jnp.zeros((LANES, LANES), f32)
        squares = [[zero for _ in at] for _ in range(2)]
        pulls = [[zero for _ in at] for _ in range(2)]
        for h in range(heads):
            carried = [dot(c_m, self.take_rows(self.fin, 0, s, h, d)) for d in range(2)]
            for i, t in enumerate(at):
                g = self.dz[s, t, lanes_of(h)].astype(f32) * self.gain[:, lanes_of(h)]
                direct = self.skip[:, h : h + 1] * self.x[s, t, lanes_of(h)].astype(f32)
                for d, grow in ((0, "grow_f"), (1, "grow_r")):
                    y = self.y[s, d, t, lanes_of(h)] + self.col(grow, s, h, t) * carried[d][i * LANES : (i + 1) * LANES]
                    y += direct
                    self.y[s, d, t, lanes_of(h)] = y
                    squares[d][i] += y * y
                    pulls[d][i] += g * y
        share = 1.0 / (heads * LANES)
        lane = iota2((LANES, LANES), 1)
        for i, t in enumerate(at):
            scale = [lax.rsqrt(jnp.sum(squares[d][i], axis=1, keepdims=True) * share + epsilon) for d in range(2)]
            means = [scale[d] * jnp.sum(pulls[d][i], axis=1, keepdims=True) * share for d in range(2)]
            pull = [scale[d] * scale[d] * means[d] for d in range(2)]
            given = [zero, zero]
            for h in range(heads):
                gain = self.gain[:, lanes_of(h)]
                g = self.dz[s, t, lanes_of(h)].astype(f32) * gain
                direct = self.skip[:, h : h + 1] * self.x[s, t, lanes_of(h)].astype(f32)
                y = [self.y[s, d, t, lanes_of(h)] for d in range(2)]
                rows = pl.ds(s * length + i * LANES, LANES)
                self.z[rows, lanes_of(h)] = ((y[0] * scale[0] + y[1] * scale[1]) * gain).astype(bf16)
                for d in range(2):
                    grad = (scale[d] * g - pull[d] * y[d]).astype(bf16)
                    self.dy[s, d, t, lanes_of(h)] = grad
                    total = jnp.sum(grad.astype(f32) * (y[d] - direct), axis=1, keepdims=True)
                    given[d] = jnp.where(lane == h, total, given[d])
            for d in range(2):
                self.cols[d, s, t] = given[d]
        for h in range(heads):
            for d, grow in ((0, "grow_f"), (1, "grow_r")):
                left = (c_t * self.row(grow, s, h)).astype(bf16)
                self.put_rows(1, s, h, d, dot(left, self.dy[s, d, :, lanes_of(h)]))

    def local_grads(self, s):
        at, state = self.blocks(), self.state
        b_m, c_m = self.bc[s, 0, :, :state], self.bc[s, 1, :, :state]
        self.scores[...] = dot(b_m, c_m, NT)
        self.dscore[s] = jnp.zeros_like(self.scores)
        d_c = jnp.zeros((self.length, state), f32)
        above = iota2((LANES, LANES), 1) - iota2((LANES, LANES), 0)
        none = jnp.zeros((LANES, LANES), bf16)
        for h in range(self.heads):
            x_h = self.x[s, :, lanes_of(h)]
            d_f, d_r = self.dy[s, 0, :, lanes_of(h)], self.dy[s, 1, :, lanes_of(h)]
            p_f, p_r = dot(x_h, d_f, NT), dot(x_h, d_r, NT)
            f_rows, r_rows = [], []
            for i, t in enumerate(at):
                low, high = self.col("low", s, h, t), self.col("high", s, h, t)
                f_cols, r_cols = [], []
                for j in range(len(at)):
                    here = slice(i * LANES, (i + 1) * LANES), slice(j * LANES, (j + 1) * LANES)
                    to_f = lambda: self.row("cum", s, h)[:, here[1]] - low
                    to_r = lambda: high - self.row("exc", s, h)[:, here[1]]
                    power = to_f() if i < j else to_r() if i > j else jnp.minimum(to_f(), to_r())
                    decay = jnp.exp(power)
                    weight = decay * self.scores[here]
                    if i < j:
                        picked = p_f[here]
                        f_cols.append(weight.astype(bf16))
                        r_cols.append(none)
                    elif i > j:
                        picked = p_r[here]
                        f_cols.append(none)
                        r_cols.append(weight.astype(bf16))
                    else:
                        picked = jnp.where(above >= 0, p_f[here], 0.0) + jnp.where(above <= 0, p_r[here], 0.0)
                        f_cols.append(jnp.where(above >= 0, weight, 0.0).astype(bf16))
                        r_cols.append(jnp.where(above <= 0, weight, 0.0).astype(bf16))
                    self.dscore[s, t, here[1]] += decay * picked
                f_rows.append(jnp.concatenate(f_cols, axis=1))
                r_rows.append(jnp.concatenate(r_cols, axis=1))
            self.y[s, 0, :, lanes_of(h)] = dot(jnp.concatenate(f_rows, axis=0), d_f)
            self.y[s, 1, :, lanes_of(h)] = dot(jnp.concatenate(r_rows, axis=0), d_r)
            whole = pl.ds(0, self.length)
            d_c += dot(d_f, self.take_rows(self.fin, 0, s, h, 0), NT) * self.col("grow_f", s, h, whole)
            d_c += dot(d_r, self.take_rows(self.fin, 0, s, h, 1), NT) * self.col("grow_r", s, h, whole)
        self.carried[s, :, :state] = d_c

    def finish_grads(self, s):
        length, heads, state = self.length, self.heads, self.state
        at = self.blocks()
        b_m, c_m = self.bc[s, 0, :, :state], self.bc[s, 1, :, :state]
        lane = iota2((LANES, LANES), 1)
        lane_row = iota2((1, LANES), 1)
        zero = jnp.zeros((LANES, LANES), f32)
        into = [[zero for _ in at] for _ in range(2)]
        total = jnp.zeros((1, LANES), f32)
        d_b = jnp.zeros((length, state), f32)
        ends = jnp.exp(self.end_row[s])
        whole = pl.ds(0, length)
        for h in range(heads):
            x_h = self.x[s, :, lanes_of(h)]
            s_f, s_r = (self.take_rows(self.fin, 0, s, h, d).astype(f32) for d in range(2))
            in_f, in_r = (self.take_rows(self.fin, 1, s, h, d) for d in range(2))
            own, own_r = (self.take_rows(self.par, d, s, h, d).astype(f32) for d in range(2))
            tail_f, tail_r = self.col("tail_f", s, h, whole), self.col("tail_r", s, h, whole)
            u_f, u_r = dot(b_m, in_f), dot(b_m, in_r)
            d_b += dot(x_h, in_f, NT) * tail_f + dot(x_h, in_r, NT) * tail_r
            for i, t in enumerate(at):
                cut = slice(i * LANES, (i + 1) * LANES)
                x = self.x[s, t, lanes_of(h)].astype(f32)
                u = [
                    self.y[s, 0, t, lanes_of(h)] + tail_f[cut] * u_f[cut],
                    self.y[s, 1, t, lanes_of(h)] + tail_r[cut] * u_r[cut],
                ]
                skipped = self.dy[s, 0, t, lanes_of(h)].astype(f32) + self.dy[s, 1, t, lanes_of(h)].astype(f32)
                rows = pl.ds(s * length + i * LANES, LANES)
                self.dx[rows, lanes_of(h)] = (u[0] + u[1] + self.skip[:, h : h + 1] * skipped).astype(bf16)
                for d in range(2):
                    into[d][i] = jnp.where(lane == h, jnp.sum(x * u[d], axis=1, keepdims=True), into[d][i])
            decay = ends[:, h : h + 1]
            a_f, a_r = in_f.astype(f32), in_r.astype(f32)
            ending = a_f * (decay * s_f + own) + s_r * (decay * a_r + own_r)
            ended = jnp.sum(jnp.sum(ending, axis=0, keepdims=True), axis=1, keepdims=True)
            total = jnp.where(lane_row == h, ended, total)
        into_f, into_r = (jnp.concatenate(rows, axis=0) for rows in into)
        d_cum = self.cols[0, s] - into_f
        d_exc = into_r - self.cols[1, s]
        upper = (iota2((length, length), 0) <= iota2((length, length), 1)).astype(bf16)
        d_la = exact_dot(upper, d_cum + d_exc, heads) - d_exc + total
        d_raw = (into_f + into_r) * self.keep[1, s] - self.keep[0, s] * d_la
        d_raw = jnp.where(iota2((length, LANES), 1) < heads, d_raw, 0.0)
        scores = self.dscore[s].astype(bf16)
        d_b += dot(scores, c_m)
        d_c = self.carried[s, :, :state] + dot(scores, b_m, TN)
        tail = jnp.concatenate([d_raw[:, : LANES - 2 * state], d_b, d_c], axis=1)
        self.tail[pl.ds(s * length, length)] = tail.astype(bf16)

    def pair(self, which, k):
        length = self.length
        lower, upper = k * CHUNK, self.width - CHUNK - k * CHUNK
        first = jnp.where(self.mine == 0, lower, upper)
        other = lower + upper - first

        def product(start):
            at = chunk_at(start)
            if which == 0:
                return dot(self.z[...], self.wo[:, at])
            return dot(self.dx[...], self.wv[at, :], NT) + dot(self.tail[...], self.side[:, at])

        kept, away = product(first), product(other)
        turned = jnp.concatenate([kept[length:], away[length:]], axis=0).astype(bf16)
        turned = dot(turned, mirror_matrix())
        snd = self.out_snd if which == 0 else self.dh_snd
        snd[k] = (away[:length] + turned[:length]).astype(bf16)
        self.mp_copy(which, k).start()
        self.hold[which, k] = kept[:length] + turned[length:]

    def settle(self, which):
        rcv, out = (self.out_rcv, self.out) if which == 0 else (self.dh_rcv, self.dh)
        for k in range(self.chunks):
            self.mp_copy(which, k).wait()
            at = jnp.where(self.mine == 0, k, self.chunks - 1 - k)
            out[:, chunk_at(at * CHUNK)] = (self.hold[which, k] + rcv[k].astype(f32)).astype(bf16)


def layer_kernel(sizes, *refs):
    layer = Layer(sizes, refs + (pltpu.get_barrier_semaphore(),))
    length, inner = layer.length, layer.inner
    hidden_load, value_load, cot_load, out_load = layer.loads()
    for load in (hidden_load, value_load, cot_load, out_load):
        load.start()
    layer.greet()
    layer.side_weights()
    hidden_load.wait()
    layer.flip_into(layer.src)
    layer.prepare()
    for s in range(2):
        layer.end_row[s] = layer.cols[0, s, length - 1 : length]
    layer.meet()
    layer.start_decays()
    value_load.wait()

    def values(s):
        def one(k, none):
            at = chunk_at(k * CHUNK)
            layer.x[s, :, at] = dot(layer.src[pl.ds(s * length, length)], layer.wv[:, at]).astype(bf16)
            return none

        lax.fori_loop(0, inner // CHUNK, one, 0)

    def output_grads(k, none):
        at = chunk_at(k * CHUNK)
        both = dot(layer.grd[...], layer.wo[at, :], NT)
        layer.dz[0, :, at] = jnp.where(known, both[:length], 0.0).astype(bf16)
        layer.dz[1, :, at] = jnp.where(known, both[length:], 0.0).astype(bf16)
        return none

    for s in range(2):
        values(s)
        layer.ends(s)
        layer.begin(0, s)
    cot_load.wait()
    layer.flip_into(layer.grd)
    layer.finish_decays()
    layer.own_decays()
    layer.spread(0, 0)
    known = jnp.where(layer.ids[...] != 4, 1.0, 0.0)
    known = jnp.broadcast_to(known, (8, length)).T[:, :1] > 0.5
    out_load.wait()
    lax.fori_loop(0, inner // CHUNK, output_grads, 0)
    layer.spread(0, 1)
    layer.local_outputs(0)
    layer.send_home(0, 0)
    layer.local_outputs(1)
    layer.send_home(0, 1)
    layer.arrive(0, 0)
    layer.finish_outputs(0)
    layer.begin(1, 0)
    layer.arrive(0, 1)
    layer.finish_outputs(1)
    layer.begin(1, 1)
    layer.spread(1, 0)
    pairs = range(layer.chunks)
    half = layer.chunks // 2
    for k in pairs[:half]:
        layer.pair(0, k)
    layer.spread(1, 1)
    for k in pairs[half:]:
        layer.pair(0, k)
    layer.send_home(1, 0)
    layer.local_grads(0)
    layer.send_home(1, 1)
    layer.local_grads(1)
    layer.arrive(1, 0)
    layer.finish_grads(0)
    layer.arrive(1, 1)
    layer.finish_grads(1)
    for k in pairs:
        layer.pair(1, k)
    layer.settle(0)
    layer.settle(1)


def per_device(
    hidden, ids, w_value, w_bc, w_step, step_bias, decay_log, skip, norm_gain, w_out, cotangent
):
    length, width = hidden.shape
    heads, inner, state = w_step.shape[1], w_value.shape[1], w_bc.shape[2] // 2
    count, parts = lax.axis_size("seq"), lax.axis_size("mp")
    assert w_bc.shape[1] == 1 and inner == heads * LANES
    group = 1
    while 4 * group * group <= count:
        group *= 2
    assert count % group == 0 and heads % group == 0 and parts == 2
    planes, each = count // group, heads // group
    rows = each * state
    share = width // parts
    chunks = share // CHUNK
    vmem, anywhere = pl.BlockSpec(memory_space=pltpu.VMEM), pl.BlockSpec(memory_space=pl.ANY)
    parcel = (2, 2, group, 2, rows, LANES)
    travel = (chunks, length, CHUNK)
    sem = pltpu.SemaphoreType.DMA
    scratch = [
        pltpu.VMEM((2 * length, width), bf16),
        pltpu.VMEM((2 * length, width), bf16),
        pltpu.VMEM(w_value.shape, bf16),
        pltpu.VMEM(w_out.shape, bf16),
        pltpu.VMEM((LANES, width), bf16),
        pltpu.VMEM((2, length, inner), bf16),
        pltpu.VMEM((2, length, inner), bf16),
        pltpu.VMEM((2, 2, length, inner), f32),
        pltpu.VMEM((2 * length, inner), bf16),
        pltpu.VMEM((2, 2, length, inner), bf16),
        pltpu.VMEM((2 * length, inner), bf16),
        pltpu.VMEM((2 * length, LANES), bf16),
        pltpu.VMEM((2, length, LANES), f32),
        pltpu.VMEM((len(COLUMNS), 2, length, LANES), f32),
        pltpu.VMEM((len(COLUMNS), 2, heads, length), f32),
        pltpu.VMEM((2, 2, length, LANES), bf16),
        pltpu.VMEM((length, length), f32),
        pltpu.VMEM((2, length, length), f32),
        pltpu.VMEM((2, length, LANES), f32),
        pltpu.VMEM((2, 2 * state, length), f32),
        pltpu.VMEM((2, 2, length, LANES), f32),
        pltpu.VMEM((2, 1, LANES), f32),
        pltpu.VMEM((1, LANES), f32),
        pltpu.VMEM((count, 1, LANES), f32),
        pltpu.VMEM((2, each, count, LANES), f32),
        pltpu.VMEM((2, each, planes, LANES), f32),
        pltpu.VMEM(parcel, bf16),
        pltpu.VMEM(parcel, bf16),
        pltpu.VMEM((2, 2, 2, rows, LANES), bf16),
        pltpu.VMEM((2, 2, planes, rows, LANES), bf16),
        pltpu.VMEM(parcel, bf16),
        pltpu.VMEM(parcel, bf16),
        pltpu.VMEM(travel, bf16),
        pltpu.VMEM(travel, bf16),
        pltpu.VMEM(travel, bf16),
        pltpu.VMEM(travel, bf16),
        pltpu.VMEM((2,) + travel, f32),
        sem((4,)),
        sem((2, count)),
        sem((2, 4, group)),
        sem((2, 4, planes)),
        sem((2, 4, group)),
        sem((2, 2, chunks)),
    ]
    sizes = (length, width, inner, heads, state, count, group, parts)
    return pl.pallas_call(
        partial(layer_kernel, sizes),
        in_specs=[anywhere] * 4 + [vmem] * 7,
        out_specs=(vmem, vmem),
        out_shape=(jax.ShapeDtypeStruct((length, share), bf16),) * 2,
        scratch_shapes=scratch,
        compiler_params=pltpu.CompilerParams(
            collective_id=0, has_side_effects=True, vmem_limit_bytes=52 * 1024 * 1024
        ),
    )(
        hidden, cotangent, w_value, w_out, ids[None], w_step.T, w_bc.reshape(width, -1).T,
        step_bias[None], decay_log[None], skip[None], norm_gain[None],
    )


def solution(mesh):
    in_specs = (
        P("seq", None),
        P("seq"),
        P(None, "mp"),
        P(None, "mp", None),
        P(None, "mp"),
        P("mp"),
        P("mp"),
        P("mp"),
        P("mp"),
        P("mp", None),
        P("seq", None),
    )
    out_specs = (P("seq", "mp"), P("seq", "mp"))
    return jax.shard_map(
        per_device, mesh=mesh, in_specs=in_specs, out_specs=out_specs, check_vma=False
    )
```

```python
from functools import partial

import jax
import jax.numpy as jnp
from jax import lax
from jax.experimental import pallas as pl
from jax.experimental.pallas import tpu as pltpu
from jax.sharding import PartitionSpec as P

f32, bf16 = jnp.float32, jnp.bfloat16
epsilon = 1e-05
LANES = 128
CHUNK = 256
STRIP = 32
NN = (((1,), (0,)), ((), ()))
NT = (((1,), (1,)), ((), ()))
TN = (((0,), (0,)), ((), ()))
MESH_ID = pl.DeviceIdType.MESH
COLUMNS = ("cum", "exc", "low", "high", "grow_f", "grow_r", "tail_f", "tail_r")

NAMES = (
    "hidden_hbm", "cot_hbm", "wv_hbm", "wo_hbm", "ids_hbm", "step_hbm", "bc_hbm", "bias_hbm",
    "decay_hbm", "skip_hbm", "gain_hbm", "out", "dh", "src", "grd", "wv", "wo", "side", "x", "g", "direct", "wide", "grown",
    "tailed", "prod", "pick", "gather", "y", "z", "dy", "dx", "tail", "aux", "cols", "rows", "bc",
    "scores", "dscore", "carried", "bct", "keep", "end_row", "dec_row", "dec_got", "dec", "plane_dec",
    "par", "got", "agg", "far", "back", "fin", "out_snd", "out_rcv", "dh_snd", "dh_rcv", "hold",
    "load_sem", "dec_sem", "go_sem", "far_sem", "home_sem", "mp_sem", "small_sem", "ids", "step_t", "bc_t", "bias",
    "decay", "skip", "gain", "barrier",
)


def dot(a, b, dims=NN):
    return lax.dot_general(a, b, dims, preferred_element_type=f32)


def iota2(shape, axis):
    return lax.broadcasted_iota(jnp.int32, shape, axis)


def mirror_matrix():
    return (iota2((CHUNK, CHUNK), 0) + iota2((CHUNK, CHUNK), 1) == CHUNK - 1).astype(bf16)


def chunk_at(start):
    return pl.ds(pl.multiple_of(start, CHUNK), CHUNK)


def lanes_of(h):
    return pl.ds(h * LANES, LANES)


def thirds(value, used):
    value = jnp.where(iota2(value.shape, 1) < used, value, 0.0)
    hi = value.astype(bf16).astype(f32)
    rest = value - hi
    mid = rest.astype(bf16).astype(f32)
    low = (rest - mid).astype(bf16).astype(f32)
    return (hi + pltpu.roll(mid, used, 1) + pltpu.roll(low, 2 * used, 1)).astype(bf16)


def exact_dot(matrix, value, used):
    result = dot(matrix, thirds(value, used))
    result += pltpu.roll(result, LANES - used, 1) + pltpu.roll(result, LANES - 2 * used, 1)
    return jnp.where(iota2(value.shape, 1) < used, result, 0.0)


class Layer:
    def __init__(self, sizes, refs):
        self.length, self.width, self.inner, self.heads, self.state, self.count, self.group, self.parts = sizes
        for name, ref in zip(NAMES, refs):
            setattr(self, name, ref)
        self.planes = self.count // self.group
        self.each = self.heads // self.group
        me = lax.axis_index("seq")
        self.me, self.plane, self.member = me, me // self.group, lax.rem(me, self.group)
        self.mine = lax.axis_index("mp")
        self.share = self.width // self.parts
        self.chunks = self.share // CHUNK

    def loads(self):
        top = self.src.at[pl.ds(0, self.length)]
        bottom = self.grd.at[pl.ds(0, self.length)]
        pairs = [(self.hidden_hbm, top), (self.wv_hbm, self.wv), (self.cot_hbm, bottom), (self.wo_hbm, self.wo)]
        return [pltpu.make_async_copy(a, b, self.load_sem.at[i]) for i, (a, b) in enumerate(pairs)]

    def small_loads(self):
        pairs = [
            (self.step_hbm, self.step_t), (self.bc_hbm, self.bc_t), (self.bias_hbm, self.bias),
            (self.decay_hbm, self.decay), (self.skip_hbm, self.skip), (self.gain_hbm, self.gain), (self.ids_hbm, self.ids),
        ]
        return [pltpu.make_async_copy(a, b, self.small_sem.at[i]) for i, (a, b) in enumerate(pairs)]

    def peer(self, hop):
        return lax.rem(self.me + hop, self.count)

    def greet(self):
        def one(hop, none):
            pl.semaphore_signal(self.barrier, inc=1, device_id={"seq": self.peer(hop)}, device_id_type=MESH_ID)
            return none

        lax.fori_loop(1, self.count, one, 0)
        pl.semaphore_signal(self.barrier, inc=1, device_id={"mp": 1 - self.mine}, device_id_type=MESH_ID)

    def meet(self):
        pl.semaphore_wait(self.barrier, self.count)

    def remote(self, src, dst, sems, where, device):
        return pltpu.make_async_remote_copy(
            src_ref=src, dst_ref=dst, send_sem=sems.at[(0,) + where], recv_sem=sems.at[(1,) + where],
            device_id=device, device_id_type=MESH_ID,
        )

    def decay_copy(self, hop):
        return self.remote(self.dec_row, self.dec_got.at[self.me], self.dec_sem, (hop,), {"seq": self.peer(hop)})

    def start_decays(self):
        def one(hop, none):
            self.decay_copy(hop).start()
            return none

        lax.fori_loop(1, self.count, one, 0)

    def finish_decays(self):
        def one(hop, none):
            self.decay_copy(hop).wait()
            return none

        lax.fori_loop(1, self.count, one, 0)

    def gather_copies(self, e, s):
        for hop in range(1, self.group):
            to = lax.rem(self.member + hop, self.group)
            yield self.remote(
                self.par.at[e, s, to], self.got.at[e, s, self.member], self.go_sem, (2 * e + s, hop),
                {"seq": self.plane * self.group + to},
            )

    def plane_copies(self, e, s):
        for hop in range(1, self.planes):
            to = lax.rem(self.plane + hop, self.planes)
            which = jnp.where(to > self.plane, e, 1 - e)
            yield self.remote(
                self.agg.at[e, s, which], self.far.at[e, s, self.plane], self.far_sem, (2 * e + s, hop),
                {"seq": to * self.group + self.member},
            )

    def home_copies(self, e, s):
        for hop in range(1, self.group):
            to = lax.rem(self.member + hop, self.group)
            yield self.remote(
                self.back.at[e, s, to], self.fin.at[e, s, self.member], self.home_sem, (2 * e + s, hop),
                {"seq": self.plane * self.group + to},
            )

    def mp_copy(self, which, k):
        snd, rcv = (self.out_snd, self.out_rcv) if which == 0 else (self.dh_snd, self.dh_rcv)
        return self.remote(snd.at[k], rcv.at[k], self.mp_sem, (which, k), {"mp": 1 - self.mine})

    def put_rows(self, e, s, h, which, value):
        at = pl.ds(h % self.each * self.state, self.state)
        self.par[e, s, h // self.each, which, at] = value.astype(bf16)

    def take_rows(self, ref, e, s, h, which):
        return ref[e, s, h // self.each, which, pl.ds(h % self.each * self.state, self.state)]

    def own_decays(self):
        self.dec_got[self.me] = self.dec_row[...]
        table = jnp.concatenate([self.dec_got[j] for j in range(self.count)], axis=0)
        lane = iota2((self.count, LANES), 1)
        for s in range(2):
            for q in range(self.each):
                head = s * self.heads + self.member * self.each + q
                picked = jnp.sum(jnp.where(lane == head, table, 0.0), axis=1, keepdims=True)
                wide = jnp.broadcast_to(picked, (self.count, LANES))
                self.dec[s, q] = wide
                for p in range(self.planes):
                    product = wide[p * self.group : p * self.group + 1]
                    for m in range(1, self.group):
                        product = product * wide[p * self.group + m : p * self.group + m + 1]
                    self.plane_dec[s, q, p : p + 1] = product

    def members(self, e, s, which, q, total, visit):
        order = range(self.group) if which == e else range(self.group - 1, -1, -1)
        at = pl.ds(q * self.state, self.state)
        for m in order:
            visit(m, at, total)
            decay = self.dec[s, q, pl.ds(self.plane * self.group + m, 1)]
            total = decay * total + self.got[e, s, m, which, at].astype(f32)
        return total

    def begin(self, e, s):
        for copy in self.gather_copies(e, s):
            copy.start()

    def spread(self, e, s):
        for copy in self.gather_copies(e, s):
            copy.wait()
        self.got[e, s, self.member] = self.par[e, s, self.member]
        self.far[e, s, self.plane] = jnp.zeros((self.each * self.state, LANES), bf16)
        for which in range(2):
            for q in range(self.each):
                total = self.members(e, s, which, q, jnp.zeros((self.state, LANES), f32), lambda m, at, total: None)
                self.agg[e, s, which, pl.ds(q * self.state, self.state)] = total.astype(bf16)
        for copy in self.plane_copies(e, s):
            copy.start()

    def send_home(self, e, s):
        for copy in self.plane_copies(e, s):
            copy.wait()
        for which in range(2):
            rising = which == e
            for q in range(self.each):
                total = jnp.zeros((self.state, LANES), f32)
                for p in range(self.planes) if rising else range(self.planes - 1, -1, -1):
                    got = self.far[e, s, p, pl.ds(q * self.state, self.state)].astype(f32)
                    longer = self.plane_dec[s, q, p : p + 1] * total + got
                    total = jnp.where(p < self.plane if rising else p > self.plane, longer, total)

                def keep(m, at, value):
                    self.back[e, s, m, which, at] = value.astype(bf16)

                self.members(e, s, which, q, total, keep)
        for copy in self.home_copies(e, s):
            copy.start()

    def arrive(self, e, s):
        for copy in self.home_copies(e, s):
            copy.wait()
        self.fin[e, s, self.member] = self.back[e, s, self.member]

    def flip_into(self, ref):
        mirror = mirror_matrix()
        for k in range(self.width // CHUNK):
            tile = ref[pl.ds(0, self.length), pl.ds(k * CHUNK, CHUNK)]
            there = pl.ds(self.width - CHUNK - k * CHUNK, CHUNK)
            ref[pl.ds(self.length, self.length), there] = dot(tile, mirror).astype(bf16)

    def constants(self):
        across = iota2((LANES, self.inner), 0), iota2((LANES, self.inner), 1) // LANES
        match = lax.rem(across[0], self.heads) == across[1]
        self.pick[...] = jnp.where(match & (across[0] < 3 * self.heads), 1.0, 0.0).astype(bf16)
        down = iota2((self.inner, LANES), 0) // LANES, iota2((self.inner, LANES), 1)
        self.gather[...] = (down[0] == down[1]).astype(bf16)

    def side_weights(self):
        gap = LANES - self.heads - 2 * self.state
        self.side[...] = jnp.concatenate(
            [self.step_t[...].astype(f32), jnp.zeros((gap, self.width), f32), self.bc_t[...].astype(f32)], axis=0
        ).astype(bf16)

    def prepare(self):
        length, heads, state, used = self.length, self.heads, self.state, 2 * self.heads
        shape = (length, LANES)
        lane = iota2(shape, 1)
        aux = dot(self.src[...], self.side[...], NT)
        self.aux[0], self.aux[1] = aux[:length], aux[length:]
        raw = jnp.where(lane < heads, aux[:length], pltpu.roll(aux[length:], heads, 1))
        spare = jnp.zeros((1, LANES - used), f32)
        bias = jnp.concatenate([self.bias[...], self.bias[...], spare], axis=1)
        rate = jnp.exp(jnp.concatenate([self.decay[...], self.decay[...], spare], axis=1))
        shifted = jnp.where(lane < used, raw + bias, 0.0)
        dt = jnp.maximum(shifted, 0.0) + jnp.log1p(jnp.exp(-jnp.abs(shifted)))
        la = jnp.where(lane < used, -rate * dt, 0.0)
        lower = (iota2((length, length), 0) >= iota2((length, length), 1)).astype(bf16)
        cum = exact_dot(lower, la, used)
        exc = cum - la
        end = cum[length - 1 : length]
        log_dt = jnp.log(jnp.maximum(dt, 1e-38))
        grow_f, grow_r = jnp.exp(cum), jnp.exp(end - exc)
        tail_f, tail_r = dt * jnp.exp(end - cum), dt * jnp.exp(exc)
        values = (cum, exc, cum - log_dt, exc + log_dt, grow_f, grow_r, tail_f, tail_r)
        for i, value in enumerate(values):
            self.cols[i, 0] = value
            self.cols[i, 1] = pltpu.roll(value, LANES - heads, 1)
            flat = value.T
            self.rows[i, 0], self.rows[i, 1] = flat[:heads], flat[heads:used]
        sig = jax.nn.sigmoid(shifted)
        ratio = jnp.where(shifted < -15.0, 1.0, sig / jnp.maximum(dt, 1e-38))
        for i, value in ((0, sig * rate), (1, ratio)):
            self.keep[i, 0] = value
            self.keep[i, 1] = pltpu.roll(value, LANES - heads, 1)
        self.dec_row[...] = jnp.exp(end)
        for s in range(2):
            rounded = self.aux[s].astype(bf16)
            b_m, c_m = rounded[:, LANES - 2 * state : LANES - state], rounded[:, LANES - state :]
            self.bc[s, 0, :, :state] = b_m
            self.bc[s, 1, :, :state] = c_m
            self.bct[s] = rounded.astype(f32).T[LANES - 2 * state :]

    def row(self, name, s, h):
        return self.rows[COLUMNS.index(name), s, pl.ds(h, 1)]

    def col(self, name, s, h, at):
        return self.cols[COLUMNS.index(name), s, at, h : h + 1]

    def ends(self, s):
        b_t = self.bct[s, : self.state]
        for h in range(self.heads):
            left = jnp.concatenate([b_t * self.row("tail_f", s, h), b_t * self.row("tail_r", s, h)], axis=0).astype(bf16)
            both = dot(left, self.x[s, :, lanes_of(h)])
            self.put_rows(0, s, h, 0, both[: self.state])
            self.put_rows(0, s, h, 1, both[self.state :])

    def blocks(self):
        return [pl.ds(k * LANES, LANES) for k in range(self.length // LANES)]

    def local_outputs(self, s):
        at, state = self.blocks(), self.state
        b_m, c_m = self.bc[s, 0, :, :state], self.bc[s, 1, :, :state]
        self.scores[...] = dot(c_m, b_m, NT)
        below = iota2((LANES, LANES), 0) - iota2((LANES, LANES), 1)
        none = jnp.zeros((LANES, LANES), bf16)
        for h in range(self.heads):
            low_rows, high_rows = [], []
            for i, t in enumerate(at):
                cum, exc = self.col("cum", s, h, t), self.col("exc", s, h, t)
                low_cols, high_cols = [], []
                for j in range(len(at)):
                    cut = slice(j * LANES, (j + 1) * LANES)
                    to_f = lambda: cum - self.row("low", s, h)[:, cut]
                    to_r = lambda: self.row("high", s, h)[:, cut] - exc
                    power = to_f() if i > j else to_r() if i < j else jnp.minimum(to_f(), to_r())
                    mix = jnp.exp(power) * self.scores[t, cut]
                    low_cols.append(none if i < j else mix.astype(bf16) if i > j else jnp.where(below >= 0, mix, 0.0).astype(bf16))
                    high_cols.append(none if i > j else mix.astype(bf16) if i < j else jnp.where(below <= 0, mix, 0.0).astype(bf16))
                low_rows.append(jnp.concatenate(low_cols, axis=1))
                high_rows.append(jnp.concatenate(high_cols, axis=1))
            both = dot(jnp.concatenate(low_rows + high_rows, axis=0), self.x[s, :, lanes_of(h)])
            direct = self.skip[:, h : h + 1] * self.x[s, :, lanes_of(h)].astype(f32)
            self.direct[s, :, lanes_of(h)] = direct
            self.y[s, 0, :, lanes_of(h)] = both[: self.length] + direct
            self.y[s, 1, :, lanes_of(h)] = both[self.length :] + direct
        for d, name in ((0, "grow_f"), (1, "grow_r")):
            self.widen(name, s, d)

    def widen(self, name, s, d):
        self.wide[s, d] = dot(thirds(self.cols[COLUMNS.index(name), s], self.heads), self.pick[...])

    def strips(self):
        return [(r, pl.ds(r, STRIP)) for r in range(0, self.length, STRIP)]

    def states(self, e, s, d):
        return jnp.concatenate([self.take_rows(self.fin, e, s, h, d) for h in range(self.heads)], axis=1)

    def finish_outputs(self, s):
        length, heads, state = self.length, self.heads, self.state
        c_m = self.bc[s, 1, :, :state]
        carried = [dot(c_m, self.states(0, s, d)) for d in range(2)]
        zero = jnp.zeros((STRIP, LANES), f32)
        share = 1.0 / (heads * LANES)
        factors = []
        for r, t in self.strips():
            squares, pulls = [zero, zero], [zero, zero]
            for h in range(heads):
                g = self.g[s, t, lanes_of(h)]
                for d in range(2):
                    here = carried[d][r : r + STRIP, h * LANES : (h + 1) * LANES]
                    y = self.y[s, d, t, lanes_of(h)] + self.wide[s, d, t, lanes_of(h)] * here
                    self.y[s, d, t, lanes_of(h)] = y
                    squares[d] += y * y
                    pulls[d] += g * y
            scale = [lax.rsqrt(jnp.sum(q, axis=1, keepdims=True) * share + epsilon) for q in squares]
            means = [scale[d] * jnp.sum(pulls[d], axis=1, keepdims=True) * share for d in range(2)]
            factors.append((scale, [scale[d] * scale[d] * means[d] for d in range(2)]))
        for (r, t), (scale, pull) in zip(self.strips(), factors):
            for h in range(heads):
                g = self.g[s, t, lanes_of(h)]
                direct = self.direct[s, t, lanes_of(h)]
                y = [self.y[s, d, t, lanes_of(h)] for d in range(2)]
                z = (y[0] * scale[0] + y[1] * scale[1]) * self.gain[:, lanes_of(h)]
                self.z[pl.ds(s * length + r, STRIP), lanes_of(h)] = z.astype(bf16)
                for d in range(2):
                    grad = (scale[d] * g - pull[d] * y[d]).astype(bf16)
                    self.dy[s, d, t, lanes_of(h)] = grad
                    grad = grad.astype(f32)
                    self.grown[s, d, t, lanes_of(h)] = (self.wide[s, d, t, lanes_of(h)] * grad).astype(bf16)
                    self.prod[s, d, t, lanes_of(h)] = (grad * (y[d] - direct)).astype(bf16)
        c_t = self.bct[s, state:].astype(bf16)
        for d in range(2):
            own = dot(c_t, self.grown[s, d])
            for h in range(heads):
                self.put_rows(1, s, h, d, own[:, h * LANES : (h + 1) * LANES])

    def between(self, s):
        for d, name in ((0, "tail_f"), (1, "tail_r")):
            self.cols[d, s] = dot(self.prod[s, d], self.gather[...])
            self.widen(name, s, d)
            self.tailed[s, d] = (self.wide[s, d] * self.x[s].astype(f32)).astype(bf16)
        carried = [dot(self.grown[s, d], self.states(0, s, d), NT) for d in range(2)]
        self.carried[s, :, : self.state] = carried[0] + carried[1]

    def local_grads(self, s):
        at, state = self.blocks(), self.state
        b_m, c_m = self.bc[s, 0, :, :state], self.bc[s, 1, :, :state]
        self.scores[...] = dot(b_m, c_m, NT)
        self.dscore[s] = jnp.zeros_like(self.scores)
        above = iota2((LANES, LANES), 1) - iota2((LANES, LANES), 0)
        none = jnp.zeros((LANES, LANES), bf16)
        for h in range(self.heads):
            x_h = self.x[s, :, lanes_of(h)]
            d_f, d_r = self.dy[s, 0, :, lanes_of(h)], self.dy[s, 1, :, lanes_of(h)]
            p_f, p_r = dot(x_h, d_f, NT), dot(x_h, d_r, NT)
            f_rows, r_rows = [], []
            for i, t in enumerate(at):
                low, high = self.col("low", s, h, t), self.col("high", s, h, t)
                f_cols, r_cols = [], []
                for j in range(len(at)):
                    here = slice(i * LANES, (i + 1) * LANES), slice(j * LANES, (j + 1) * LANES)
                    to_f = lambda: self.row("cum", s, h)[:, here[1]] - low
                    to_r = lambda: high - self.row("exc", s, h)[:, here[1]]
                    power = to_f() if i < j else to_r() if i > j else jnp.minimum(to_f(), to_r())
                    decay = jnp.exp(power)
                    weight = decay * self.scores[here]
                    if i < j:
                        picked = p_f[here]
                        f_cols.append(weight.astype(bf16))
                        r_cols.append(none)
                    elif i > j:
                        picked = p_r[here]
                        f_cols.append(none)
                        r_cols.append(weight.astype(bf16))
                    else:
                        picked = jnp.where(above >= 0, p_f[here], 0.0) + jnp.where(above <= 0, p_r[here], 0.0)
                        f_cols.append(jnp.where(above >= 0, weight, 0.0).astype(bf16))
                        r_cols.append(jnp.where(above <= 0, weight, 0.0).astype(bf16))
                    self.dscore[s, t, here[1]] += decay * picked
                f_rows.append(jnp.concatenate(f_cols, axis=1))
                r_rows.append(jnp.concatenate(r_cols, axis=1))
            self.y[s, 0, :, lanes_of(h)] = dot(jnp.concatenate(f_rows, axis=0), d_f)
            self.y[s, 1, :, lanes_of(h)] = dot(jnp.concatenate(r_rows, axis=0), d_r)

    def finish_grads(self, s):
        length, heads, state = self.length, self.heads, self.state
        b_m, c_m = self.bc[s, 0, :, :state], self.bc[s, 1, :, :state]
        lane_row = iota2((1, LANES), 1)
        total = jnp.zeros((1, LANES), f32)
        ends = jnp.exp(self.end_row[s])
        inward = [self.states(1, s, d) for d in range(2)]
        carried = [dot(b_m, inward[d]) for d in range(2)]
        for r, t in self.strips():
            for h in range(heads):
                x = self.x[s, t, lanes_of(h)].astype(f32)
                skipped = self.dy[s, 0, t, lanes_of(h)].astype(f32) + self.dy[s, 1, t, lanes_of(h)].astype(f32)
                dx = self.skip[:, h : h + 1] * skipped
                for d in range(2):
                    here = carried[d][r : r + STRIP, h * LANES : (h + 1) * LANES]
                    u = self.y[s, d, t, lanes_of(h)] + self.wide[s, d, t, lanes_of(h)] * here
                    dx += u
                    self.prod[s, d, t, lanes_of(h)] = (x * u).astype(bf16)
                self.dx[pl.ds(s * length + r, STRIP), lanes_of(h)] = dx.astype(bf16)
        d_b = dot(self.tailed[s, 0], inward[0], NT) + dot(self.tailed[s, 1], inward[1], NT)
        for h in range(heads):
            s_f, s_r = (self.take_rows(self.fin, 0, s, h, d).astype(f32) for d in range(2))
            a_f, a_r = (self.take_rows(self.fin, 1, s, h, d).astype(f32) for d in range(2))
            own, own_r = (self.take_rows(self.par, d, s, h, d).astype(f32) for d in range(2))
            decay = ends[:, h : h + 1]
            ending = a_f * (decay * s_f + own) + s_r * (decay * a_r + own_r)
            ended = jnp.sum(jnp.sum(ending, axis=0, keepdims=True), axis=1, keepdims=True)
            total = jnp.where(lane_row == h, ended, total)
        into_f, into_r = (dot(self.prod[s, d], self.gather[...]) for d in range(2))
        d_cum = self.cols[0, s] - into_f
        d_exc = into_r - self.cols[1, s]
        upper = (iota2((length, length), 0) <= iota2((length, length), 1)).astype(bf16)
        d_la = exact_dot(upper, d_cum + d_exc, heads) - d_exc + total
        d_raw = (into_f + into_r) * self.keep[1, s] - self.keep[0, s] * d_la
        d_raw = jnp.where(iota2((length, LANES), 1) < heads, d_raw, 0.0)
        scores = self.dscore[s].astype(bf16)
        d_b += dot(scores, c_m)
        d_c = self.carried[s, :, :state] + dot(scores, b_m, TN)
        tail = jnp.concatenate([d_raw[:, : LANES - 2 * state], d_b, d_c], axis=1)
        self.tail[pl.ds(s * length, length)] = tail.astype(bf16)

    def pair(self, which, k):
        length = self.length
        lower, upper = k * CHUNK, self.width - CHUNK - k * CHUNK
        first = jnp.where(self.mine == 0, lower, upper)
        other = lower + upper - first

        def product(start):
            at = chunk_at(start)
            if which == 0:
                return dot(self.z[...], self.wo[:, at])
            return dot(self.dx[...], self.wv[at, :], NT) + dot(self.tail[...], self.side[:, at])

        kept, away = product(first), product(other)
        turned = jnp.concatenate([kept[length:], away[length:]], axis=0).astype(bf16)
        turned = dot(turned, mirror_matrix())
        snd = self.out_snd if which == 0 else self.dh_snd
        snd[k] = (away[:length] + turned[:length]).astype(bf16)
        self.mp_copy(which, k).start()
        self.hold[which, k] = kept[:length] + turned[length:]

    def settle(self, which):
        rcv, out = (self.out_rcv, self.out) if which == 0 else (self.dh_rcv, self.dh)
        for k in range(self.chunks):
            self.mp_copy(which, k).wait()
            at = jnp.where(self.mine == 0, k, self.chunks - 1 - k)
            out[:, chunk_at(at * CHUNK)] = (self.hold[which, k] + rcv[k].astype(f32)).astype(bf16)


def layer_kernel(sizes, *refs):
    layer = Layer(sizes, refs + (pltpu.get_barrier_semaphore(),))
    length, inner = layer.length, layer.inner
    hidden_load, value_load, cot_load, out_load = layer.loads()
    small_loads = layer.small_loads()
    for load in [hidden_load] + small_loads + [value_load, cot_load, out_load]:
        load.start()
    layer.greet()
    layer.constants()
    for load in small_loads:
        load.wait()
    layer.side_weights()
    hidden_load.wait()
    layer.flip_into(layer.src)
    layer.prepare()
    for s in range(2):
        layer.end_row[s] = layer.cols[0, s, length - 1 : length]
    layer.meet()
    layer.start_decays()
    value_load.wait()

    def values(s):
        def one(k, none):
            at = chunk_at(k * CHUNK)
            layer.x[s, :, at] = dot(layer.src[pl.ds(s * length, length)], layer.wv[:, at]).astype(bf16)
            return none

        lax.fori_loop(0, inner // CHUNK, one, 0)

    def output_grads(k, none):
        at = chunk_at(k * CHUNK)
        both = dot(layer.grd[...], layer.wo[at, :], NT)
        for s in range(2):
            dz = jnp.where(known, both[s * length : (s + 1) * length], 0.0).astype(bf16)
            layer.g[s, :, at] = dz.astype(f32) * layer.gain[:, at]
        return none

    for s in range(2):
        values(s)
        layer.ends(s)
        layer.begin(0, s)
    cot_load.wait()
    layer.flip_into(layer.grd)
    layer.finish_decays()
    layer.own_decays()
    layer.spread(0, 0)
    known = jnp.where(layer.ids[...] != 4, 1.0, 0.0)
    known = jnp.broadcast_to(known, (8, length)).T[:, :1] > 0.5
    out_load.wait()
    lax.fori_loop(0, inner // CHUNK, output_grads, 0)
    layer.spread(0, 1)
    layer.local_outputs(0)
    layer.send_home(0, 0)
    layer.local_outputs(1)
    layer.send_home(0, 1)
    layer.arrive(0, 0)
    layer.finish_outputs(0)
    layer.begin(1, 0)
    layer.arrive(0, 1)
    layer.finish_outputs(1)
    layer.begin(1, 1)
    layer.between(0)
    layer.spread(1, 0)
    pairs = range(layer.chunks)
    half = layer.chunks // 2
    for k in pairs[:half]:
        layer.pair(0, k)
    layer.spread(1, 1)
    for k in pairs[half:]:
        layer.pair(0, k)
    layer.send_home(1, 0)
    layer.local_grads(0)
    layer.between(1)
    layer.send_home(1, 1)
    layer.local_grads(1)
    layer.arrive(1, 0)
    layer.finish_grads(0)
    layer.arrive(1, 1)
    layer.finish_grads(1)
    for k in pairs:
        layer.pair(1, k)
    layer.settle(0)
    layer.settle(1)


def per_device(
    hidden, ids, w_value, w_bc, w_step, step_bias, decay_log, skip, norm_gain, w_out, cotangent
):
    length, width = hidden.shape
    heads, inner, state = w_step.shape[1], w_value.shape[1], w_bc.shape[2] // 2
    count, parts = lax.axis_size("seq"), lax.axis_size("mp")
    assert w_bc.shape[1] == 1 and inner == heads * LANES
    group = 1
    while 4 * group * group <= count:
        group *= 2
    assert count % group == 0 and heads % group == 0 and parts == 2
    planes, each = count // group, heads // group
    rows = each * state
    share = width // parts
    chunks = share // CHUNK
    vmem, hbm = pl.BlockSpec(memory_space=pltpu.VMEM), pl.BlockSpec(memory_space=pltpu.HBM)
    parcel = (2, 2, group, 2, rows, LANES)
    travel = (chunks, length, CHUNK)
    sem = pltpu.SemaphoreType.DMA
    scratch = [
        pltpu.VMEM((2 * length, width), bf16),
        pltpu.VMEM((2 * length, width), bf16),
        pltpu.VMEM(w_value.shape, bf16),
        pltpu.VMEM(w_out.shape, bf16),
        pltpu.VMEM((LANES, width), bf16),
        pltpu.VMEM((2, length, inner), bf16),
        pltpu.VMEM((2, length, inner), f32),
        pltpu.VMEM((2, length, inner), f32),
        pltpu.VMEM((2, 2, length, inner), f32),
        pltpu.VMEM((2, 2, length, inner), bf16),
        pltpu.VMEM((2, 2, length, inner), bf16),
        pltpu.VMEM((2, 2, length, inner), bf16),
        pltpu.VMEM((LANES, inner), bf16),
        pltpu.VMEM((inner, LANES), bf16),
        pltpu.VMEM((2, 2, length, inner), f32),
        pltpu.VMEM((2 * length, inner), bf16),
        pltpu.VMEM((2, 2, length, inner), bf16),
        pltpu.VMEM((2 * length, inner), bf16),
        pltpu.VMEM((2 * length, LANES), bf16),
        pltpu.VMEM((2, length, LANES), f32),
        pltpu.VMEM((len(COLUMNS), 2, length, LANES), f32),
        pltpu.VMEM((len(COLUMNS), 2, heads, length), f32),
        pltpu.VMEM((2, 2, length, LANES), bf16),
        pltpu.VMEM((length, length), f32),
        pltpu.VMEM((2, length, length), f32),
        pltpu.VMEM((2, length, LANES), f32),
        pltpu.VMEM((2, 2 * state, length), f32),
        pltpu.VMEM((2, 2, length, LANES), f32),
        pltpu.VMEM((2, 1, LANES), f32),
        pltpu.VMEM((1, LANES), f32),
        pltpu.VMEM((count, 1, LANES), f32),
        pltpu.VMEM((2, each, count, LANES), f32),
        pltpu.VMEM((2, each, planes, LANES), f32),
        pltpu.VMEM(parcel, bf16),
        pltpu.VMEM(parcel, bf16),
        pltpu.VMEM((2, 2, 2, rows, LANES), bf16),
        pltpu.VMEM((2, 2, planes, rows, LANES), bf16),
        pltpu.VMEM(parcel, bf16),
        pltpu.VMEM(parcel, bf16),
        pltpu.VMEM(travel, bf16),
        pltpu.VMEM(travel, bf16),
        pltpu.VMEM(travel, bf16),
        pltpu.VMEM(travel, bf16),
        pltpu.VMEM((2,) + travel, f32),
        sem((4,)),
        sem((2, count)),
        sem((2, 4, group)),
        sem((2, 4, planes)),
        sem((2, 4, group)),
        sem((2, 2, chunks)),
        sem((7,)),
        pltpu.VMEM((1, length), jnp.int32),
        pltpu.VMEM((heads, width), bf16),
        pltpu.VMEM((2 * state, width), bf16),
        pltpu.VMEM((1, heads), f32),
        pltpu.VMEM((1, heads), f32),
        pltpu.VMEM((1, heads), f32),
        pltpu.VMEM((1, inner), f32),
    ]
    sizes = (length, width, inner, heads, state, count, group, parts)
    return pl.pallas_call(
        partial(layer_kernel, sizes),
        in_specs=[hbm] * 11,
        out_specs=(vmem, vmem),
        out_shape=(jax.ShapeDtypeStruct((length, share), bf16),) * 2,
        scratch_shapes=scratch,
        compiler_params=pltpu.CompilerParams(
            collective_id=0, has_side_effects=True, vmem_limit_bytes=52 * 1024 * 1024
        ),
    )(
        *(
            pltpu.with_memory_space_constraint(value, pltpu.HBM)
            for value in (
                hidden, cotangent, w_value, w_out, ids[None], w_step.T, w_bc.reshape(width, -1).T,
                step_bias[None], decay_log[None], skip[None], norm_gain[None],
            )
        )
    )


def solution(mesh):
    in_specs = (
        P("seq", None),
        P("seq"),
        P(None, "mp"),
        P(None, "mp", None),
        P(None, "mp"),
        P("mp"),
        P("mp"),
        P("mp"),
        P("mp"),
        P("mp", None),
        P("seq", None),
    )
    out_specs = (P("seq", "mp"), P("seq", "mp"))
    return jax.shard_map(
        per_device, mesh=mesh, in_specs=in_specs, out_specs=out_specs, check_vma=False
    )
```

```python
from functools import partial

import jax
import jax.numpy as jnp
from jax import lax
from jax.experimental import pallas as pl
from jax.experimental.pallas import tpu as pltpu
from jax.sharding import PartitionSpec as P

f32, bf16 = jnp.float32, jnp.bfloat16
epsilon = 1e-05
LANES = 128
CHUNK = 256
STRIP = 32
NN = (((1,), (0,)), ((), ()))
NT = (((1,), (1,)), ((), ()))
TN = (((0,), (0,)), ((), ()))
MESH_ID = pl.DeviceIdType.MESH
COLUMNS = ("cum", "exc", "low", "high", "grow_f", "grow_r", "tail_f", "tail_r")

NAMES = (
    "hidden_hbm", "cot_hbm", "wv_hbm", "wo_hbm", "ids_hbm", "step_hbm", "bc_hbm", "bias_hbm",
    "decay_hbm", "skip_hbm", "gain_hbm", "out", "dh", "src", "grd", "wv", "wo", "side", "x", "g", "direct", "wide", "grown",
    "tailed", "prod", "pick", "gather", "y", "z", "dy", "dx", "tail", "aux", "cols", "rows", "bc",
    "scores", "dscore", "carried", "bct", "keep", "end_row", "dec_row", "dec_got", "dec", "plane_dec",
    "par", "got", "agg", "far", "back", "fin", "out_snd", "out_rcv", "dh_snd", "dh_rcv", "hold",
    "load_sem", "dec_sem", "go_sem", "far_sem", "home_sem", "mp_sem", "small_sem", "ids", "step_t", "bc_t", "bias",
    "decay", "skip", "gain", "barrier",
)


def dot(a, b, dims=NN):
    return lax.dot_general(a, b, dims, preferred_element_type=f32)


def iota2(shape, axis):
    return lax.broadcasted_iota(jnp.int32, shape, axis)


def mirror_matrix():
    return (iota2((CHUNK, CHUNK), 0) + iota2((CHUNK, CHUNK), 1) == CHUNK - 1).astype(bf16)


def chunk_at(start):
    return pl.ds(pl.multiple_of(start, CHUNK), CHUNK)


def lanes_of(h):
    return pl.ds(h * LANES, LANES)


def thirds(value, used):
    value = jnp.where(iota2(value.shape, 1) < used, value, 0.0)
    hi = value.astype(bf16).astype(f32)
    rest = value - hi
    mid = rest.astype(bf16).astype(f32)
    low = (rest - mid).astype(bf16).astype(f32)
    return (hi + pltpu.roll(mid, used, 1) + pltpu.roll(low, 2 * used, 1)).astype(bf16)


def exact_dot(matrix, value, used):
    result = dot(matrix, thirds(value, used))
    result += pltpu.roll(result, LANES - used, 1) + pltpu.roll(result, LANES - 2 * used, 1)
    return jnp.where(iota2(value.shape, 1) < used, result, 0.0)


class Layer:
    def __init__(self, sizes, refs):
        self.length, self.width, self.inner, self.heads, self.state, self.count, self.group, self.parts = sizes
        for name, ref in zip(NAMES, refs):
            setattr(self, name, ref)
        self.planes = self.count // self.group
        self.each = self.heads // self.group
        me = lax.axis_index("seq")
        self.me, self.plane, self.member = me, me // self.group, lax.rem(me, self.group)
        self.mine = lax.axis_index("mp")
        self.share = self.width // self.parts
        self.chunks = self.share // CHUNK

    def loads(self):
        top = self.src.at[pl.ds(0, self.length)]
        bottom = self.grd.at[pl.ds(0, self.length)]
        pairs = [(self.hidden_hbm, top), (self.wv_hbm, self.wv), (self.cot_hbm, bottom), (self.wo_hbm, self.wo)]
        return [pltpu.make_async_copy(a, b, self.load_sem.at[i]) for i, (a, b) in enumerate(pairs)]

    def small_loads(self):
        pairs = [
            (self.step_hbm, self.step_t), (self.bc_hbm, self.bc_t), (self.bias_hbm, self.bias),
            (self.decay_hbm, self.decay), (self.skip_hbm, self.skip), (self.gain_hbm, self.gain), (self.ids_hbm, self.ids),
        ]
        return [pltpu.make_async_copy(a, b, self.small_sem.at[i]) for i, (a, b) in enumerate(pairs)]

    def peer(self, hop):
        return lax.rem(self.me + hop, self.count)

    def greet(self):
        def one(hop, none):
            pl.semaphore_signal(self.barrier, inc=1, device_id={"seq": self.peer(hop)}, device_id_type=MESH_ID)
            return none

        lax.fori_loop(1, self.count, one, 0)
        pl.semaphore_signal(self.barrier, inc=1, device_id={"mp": 1 - self.mine}, device_id_type=MESH_ID)

    def meet(self):
        pl.semaphore_wait(self.barrier, self.count)

    def remote(self, src, dst, sems, where, device):
        return pltpu.make_async_remote_copy(
            src_ref=src, dst_ref=dst, send_sem=sems.at[(0,) + where], recv_sem=sems.at[(1,) + where],
            device_id=device, device_id_type=MESH_ID,
        )

    def decay_copy(self, plane_hop, member_hop):
        plane = lax.rem(self.plane + plane_hop, self.planes)
        to = plane * self.group + lax.rem(self.member + member_hop, self.group)
        return self.remote(self.dec_row, self.dec_got.at[self.me], self.dec_sem, (plane_hop, member_hop), {"seq": to})

    def near_decays(self):
        return [self.decay_copy(0, m) for m in range(1, self.group)]

    def far_decays(self):
        return [self.decay_copy(p, m) for p in range(1, self.planes) for m in range(self.group)]

    def gather_copies(self, e, s):
        for hop in range(1, self.group):
            to = lax.rem(self.member + hop, self.group)
            yield self.remote(
                self.par.at[e, s, to], self.got.at[e, s, self.member], self.go_sem, (2 * e + s, hop),
                {"seq": self.plane * self.group + to},
            )

    def plane_copies(self, e, s):
        for hop in range(1, self.planes):
            to = lax.rem(self.plane + hop, self.planes)
            which = jnp.where(to > self.plane, e, 1 - e)
            yield self.remote(
                self.agg.at[e, s, which], self.far.at[e, s, self.plane], self.far_sem, (2 * e + s, hop),
                {"seq": to * self.group + self.member},
            )

    def home_copies(self, e, s):
        for hop in range(1, self.group):
            to = lax.rem(self.member + hop, self.group)
            yield self.remote(
                self.back.at[e, s, to], self.fin.at[e, s, self.member], self.home_sem, (2 * e + s, hop),
                {"seq": self.plane * self.group + to},
            )

    def mp_copy(self, which, k):
        snd, rcv = (self.out_snd, self.out_rcv) if which == 0 else (self.dh_snd, self.dh_rcv)
        return self.remote(snd.at[k], rcv.at[k], self.mp_sem, (which, k), {"mp": 1 - self.mine})

    def put_rows(self, e, s, h, which, value):
        at = pl.ds(h % self.each * self.state, self.state)
        self.par[e, s, h // self.each, which, at] = value.astype(bf16)

    def take_rows(self, ref, e, s, h, which):
        return ref[e, s, h // self.each, which, pl.ds(h % self.each * self.state, self.state)]

    def decays_of(self, rows, s, q):
        table = jnp.concatenate(rows, axis=0)
        head = s * self.heads + self.member * self.each + q
        picked = jnp.sum(jnp.where(iota2(table.shape, 1) == head, table, 0.0), axis=1, keepdims=True)
        return jnp.broadcast_to(picked, table.shape)

    def take_near(self):
        for copy in self.near_decays():
            copy.wait()
        self.dec_got[self.me] = self.dec_row[...]
        rows = [self.dec_got[self.plane * self.group + m] for m in range(self.group)]
        for s in range(2):
            for q in range(self.each):
                self.dec[s, q] = self.decays_of(rows, s, q)

    def take_far(self):
        for copy in self.far_decays():
            copy.wait()
        rows = [self.dec_got[j] for j in range(self.count)]
        for s in range(2):
            for q in range(self.each):
                wide = self.decays_of(rows, s, q)
                for p in range(self.planes):
                    product = wide[p * self.group : p * self.group + 1]
                    for m in range(1, self.group):
                        product = product * wide[p * self.group + m : p * self.group + m + 1]
                    self.plane_dec[s, q, p : p + 1] = product

    def members(self, e, s, which, q, total, visit):
        order = range(self.group) if which == e else range(self.group - 1, -1, -1)
        at = pl.ds(q * self.state, self.state)
        for m in order:
            visit(m, at, total)
            total = self.dec[s, q, m : m + 1] * total + self.got[e, s, m, which, at].astype(f32)
        return total

    def begin(self, e, s):
        for copy in self.gather_copies(e, s):
            copy.start()

    def spread(self, e, s):
        for copy in self.gather_copies(e, s):
            copy.wait()
        self.got[e, s, self.member] = self.par[e, s, self.member]
        self.far[e, s, self.plane] = jnp.zeros((self.each * self.state, LANES), bf16)
        for which in range(2):
            for q in range(self.each):
                total = self.members(e, s, which, q, jnp.zeros((self.state, LANES), f32), lambda m, at, total: None)
                self.agg[e, s, which, pl.ds(q * self.state, self.state)] = total.astype(bf16)
        for copy in self.plane_copies(e, s):
            copy.start()

    def send_home(self, e, s):
        for copy in self.plane_copies(e, s):
            copy.wait()
        for which in range(2):
            rising = which == e
            for q in range(self.each):
                total = jnp.zeros((self.state, LANES), f32)
                for p in range(self.planes) if rising else range(self.planes - 1, -1, -1):
                    got = self.far[e, s, p, pl.ds(q * self.state, self.state)].astype(f32)
                    longer = self.plane_dec[s, q, p : p + 1] * total + got
                    total = jnp.where(p < self.plane if rising else p > self.plane, longer, total)

                def keep(m, at, value):
                    self.back[e, s, m, which, at] = value.astype(bf16)

                self.members(e, s, which, q, total, keep)
        for copy in self.home_copies(e, s):
            copy.start()

    def arrive(self, e, s):
        for copy in self.home_copies(e, s):
            copy.wait()
        self.fin[e, s, self.member] = self.back[e, s, self.member]

    def flip_into(self, ref):
        mirror = mirror_matrix()
        for k in range(self.width // CHUNK):
            tile = ref[pl.ds(0, self.length), pl.ds(k * CHUNK, CHUNK)]
            there = pl.ds(self.width - CHUNK - k * CHUNK, CHUNK)
            ref[pl.ds(self.length, self.length), there] = dot(tile, mirror).astype(bf16)

    def constants(self):
        across = iota2((LANES, self.inner), 0), iota2((LANES, self.inner), 1) // LANES
        match = lax.rem(across[0], self.heads) == across[1]
        self.pick[...] = jnp.where(match & (across[0] < 3 * self.heads), 1.0, 0.0).astype(bf16)
        down = iota2((self.inner, LANES), 0) // LANES, iota2((self.inner, LANES), 1)
        self.gather[...] = (down[0] == down[1]).astype(bf16)

    def side_weights(self):
        gap = LANES - self.heads - 2 * self.state
        self.side[...] = jnp.concatenate(
            [self.step_t[...].astype(f32), jnp.zeros((gap, self.width), f32), self.bc_t[...].astype(f32)], axis=0
        ).astype(bf16)

    def prepare(self):
        length, heads, state, used = self.length, self.heads, self.state, 2 * self.heads
        shape = (length, LANES)
        lane = iota2(shape, 1)
        aux = dot(self.src[...], self.side[...], NT)
        self.aux[0], self.aux[1] = aux[:length], aux[length:]
        raw = jnp.where(lane < heads, aux[:length], pltpu.roll(aux[length:], heads, 1))
        spare = jnp.zeros((1, LANES - used), f32)
        bias = jnp.concatenate([self.bias[...], self.bias[...], spare], axis=1)
        rate = jnp.exp(jnp.concatenate([self.decay[...], self.decay[...], spare], axis=1))
        shifted = jnp.where(lane < used, raw + bias, 0.0)
        dt = jnp.maximum(shifted, 0.0) + jnp.log1p(jnp.exp(-jnp.abs(shifted)))
        la = jnp.where(lane < used, -rate * dt, 0.0)
        lower = (iota2((length, length), 0) >= iota2((length, length), 1)).astype(bf16)
        cum = exact_dot(lower, la, used)
        exc = cum - la
        end = cum[length - 1 : length]
        log_dt = jnp.log(jnp.maximum(dt, 1e-38))
        grow_f, grow_r = jnp.exp(cum), jnp.exp(end - exc)
        tail_f, tail_r = dt * jnp.exp(end - cum), dt * jnp.exp(exc)
        values = (cum, exc, cum - log_dt, exc + log_dt, grow_f, grow_r, tail_f, tail_r)
        for i, value in enumerate(values):
            self.cols[i, 0] = value
            self.cols[i, 1] = pltpu.roll(value, LANES - heads, 1)
            flat = value.T
            self.rows[i, 0], self.rows[i, 1] = flat[:heads], flat[heads:used]
        sig = jax.nn.sigmoid(shifted)
        ratio = jnp.where(shifted < -15.0, 1.0, sig / jnp.maximum(dt, 1e-38))
        for i, value in ((0, sig * rate), (1, ratio)):
            self.keep[i, 0] = value
            self.keep[i, 1] = pltpu.roll(value, LANES - heads, 1)
        self.dec_row[...] = jnp.exp(end)
        for s in range(2):
            rounded = self.aux[s].astype(bf16)
            b_m, c_m = rounded[:, LANES - 2 * state : LANES - state], rounded[:, LANES - state :]
            self.bc[s, 0, :, :state] = b_m
            self.bc[s, 1, :, :state] = c_m
            self.bct[s] = rounded.astype(f32).T[LANES - 2 * state :]

    def row(self, name, s, h):
        return self.rows[COLUMNS.index(name), s, pl.ds(h, 1)]

    def col(self, name, s, h, at):
        return self.cols[COLUMNS.index(name), s, at, h : h + 1]

    def ends(self, s):
        b_t = self.bct[s, : self.state]
        for h in range(self.heads):
            left = jnp.concatenate([b_t * self.row("tail_f", s, h), b_t * self.row("tail_r", s, h)], axis=0).astype(bf16)
            both = dot(left, self.x[s, :, lanes_of(h)])
            self.put_rows(0, s, h, 0, both[: self.state])
            self.put_rows(0, s, h, 1, both[self.state :])

    def blocks(self):
        return [pl.ds(k * LANES, LANES) for k in range(self.length // LANES)]

    def local_outputs(self, s):
        at, state = self.blocks(), self.state
        b_m, c_m = self.bc[s, 0, :, :state], self.bc[s, 1, :, :state]
        self.scores[...] = dot(c_m, b_m, NT)
        below = iota2((LANES, LANES), 0) - iota2((LANES, LANES), 1)
        none = jnp.zeros((LANES, LANES), bf16)
        for h in range(self.heads):
            low_rows, high_rows = [], []
            for i, t in enumerate(at):
                cum, exc = self.col("cum", s, h, t), self.col("exc", s, h, t)
                low_cols, high_cols = [], []
                for j in range(len(at)):
                    cut = slice(j * LANES, (j + 1) * LANES)
                    to_f = lambda: cum - self.row("low", s, h)[:, cut]
                    to_r = lambda: self.row("high", s, h)[:, cut] - exc
                    power = to_f() if i > j else to_r() if i < j else jnp.minimum(to_f(), to_r())
                    mix = jnp.exp(power) * self.scores[t, cut]
                    low_cols.append(none if i < j else mix.astype(bf16) if i > j else jnp.where(below >= 0, mix, 0.0).astype(bf16))
                    high_cols.append(none if i > j else mix.astype(bf16) if i < j else jnp.where(below <= 0, mix, 0.0).astype(bf16))
                low_rows.append(jnp.concatenate(low_cols, axis=1))
                high_rows.append(jnp.concatenate(high_cols, axis=1))
            both = dot(jnp.concatenate(low_rows + high_rows, axis=0), self.x[s, :, lanes_of(h)])
            direct = self.skip[:, h : h + 1] * self.x[s, :, lanes_of(h)].astype(f32)
            self.direct[s, :, lanes_of(h)] = direct
            self.y[s, 0, :, lanes_of(h)] = both[: self.length] + direct
            self.y[s, 1, :, lanes_of(h)] = both[self.length :] + direct
        for d, name in ((0, "grow_f"), (1, "grow_r")):
            self.widen(name, s, d)

    def widen(self, name, s, d):
        self.wide[s, d] = dot(thirds(self.cols[COLUMNS.index(name), s], self.heads), self.pick[...])

    def strips(self):
        return [(r, pl.ds(r, STRIP)) for r in range(0, self.length, STRIP)]

    def states(self, e, s, d):
        return jnp.concatenate([self.take_rows(self.fin, e, s, h, d) for h in range(self.heads)], axis=1)

    def finish_outputs(self, s):
        length, heads, state = self.length, self.heads, self.state
        c_m = self.bc[s, 1, :, :state]
        carried = [dot(c_m, self.states(0, s, d)) for d in range(2)]
        zero = jnp.zeros((STRIP, LANES), f32)
        share = 1.0 / (heads * LANES)
        factors = []
        for r, t in self.strips():
            squares, pulls = [zero, zero], [zero, zero]
            for h in range(heads):
                g = self.g[s, t, lanes_of(h)]
                for d in range(2):
                    here = carried[d][r : r + STRIP, h * LANES : (h + 1) * LANES]
                    y = self.y[s, d, t, lanes_of(h)] + self.wide[s, d, t, lanes_of(h)] * here
                    self.y[s, d, t, lanes_of(h)] = y
                    squares[d] += y * y
                    pulls[d] += g * y
            scale = [lax.rsqrt(jnp.sum(q, axis=1, keepdims=True) * share + epsilon) for q in squares]
            means = [scale[d] * jnp.sum(pulls[d], axis=1, keepdims=True) * share for d in range(2)]
            factors.append((scale, [scale[d] * scale[d] * means[d] for d in range(2)]))
        for (r, t), (scale, pull) in zip(self.strips(), factors):
            for h in range(heads):
                g = self.g[s, t, lanes_of(h)]
                direct = self.direct[s, t, lanes_of(h)]
                y = [self.y[s, d, t, lanes_of(h)] for d in range(2)]
                z = (y[0] * scale[0] + y[1] * scale[1]) * self.gain[:, lanes_of(h)]
                self.z[pl.ds(s * length + r, STRIP), lanes_of(h)] = z.astype(bf16)
                for d in range(2):
                    grad = (scale[d] * g - pull[d] * y[d]).astype(bf16)
                    self.dy[s, d, t, lanes_of(h)] = grad
                    grad = grad.astype(f32)
                    self.grown[s, d, t, lanes_of(h)] = (self.wide[s, d, t, lanes_of(h)] * grad).astype(bf16)
                    self.prod[s, d, t, lanes_of(h)] = (grad * (y[d] - direct)).astype(bf16)
        c_t = self.bct[s, state:].astype(bf16)
        for d in range(2):
            own = dot(c_t, self.grown[s, d])
            for h in range(heads):
                self.put_rows(1, s, h, d, own[:, h * LANES : (h + 1) * LANES])

    def between(self, s):
        for d, name in ((0, "tail_f"), (1, "tail_r")):
            self.cols[d, s] = dot(self.prod[s, d], self.gather[...])
            self.widen(name, s, d)
            self.tailed[s, d] = (self.wide[s, d] * self.x[s].astype(f32)).astype(bf16)
        carried = [dot(self.grown[s, d], self.states(0, s, d), NT) for d in range(2)]
        self.carried[s, :, : self.state] = carried[0] + carried[1]

    def local_grads(self, s):
        at, state = self.blocks(), self.state
        b_m, c_m = self.bc[s, 0, :, :state], self.bc[s, 1, :, :state]
        self.scores[...] = dot(b_m, c_m, NT)
        self.dscore[s] = jnp.zeros_like(self.scores)
        above = iota2((LANES, LANES), 1) - iota2((LANES, LANES), 0)
        none = jnp.zeros((LANES, LANES), bf16)
        for h in range(self.heads):
            x_h = self.x[s, :, lanes_of(h)]
            d_f, d_r = self.dy[s, 0, :, lanes_of(h)], self.dy[s, 1, :, lanes_of(h)]
            p_f, p_r = dot(x_h, d_f, NT), dot(x_h, d_r, NT)
            f_rows, r_rows = [], []
            for i, t in enumerate(at):
                low, high = self.col("low", s, h, t), self.col("high", s, h, t)
                f_cols, r_cols = [], []
                for j in range(len(at)):
                    here = slice(i * LANES, (i + 1) * LANES), slice(j * LANES, (j + 1) * LANES)
                    to_f = lambda: self.row("cum", s, h)[:, here[1]] - low
                    to_r = lambda: high - self.row("exc", s, h)[:, here[1]]
                    power = to_f() if i < j else to_r() if i > j else jnp.minimum(to_f(), to_r())
                    decay = jnp.exp(power)
                    weight = decay * self.scores[here]
                    if i < j:
                        picked = p_f[here]
                        f_cols.append(weight.astype(bf16))
                        r_cols.append(none)
                    elif i > j:
                        picked = p_r[here]
                        f_cols.append(none)
                        r_cols.append(weight.astype(bf16))
                    else:
                        picked = jnp.where(above >= 0, p_f[here], 0.0) + jnp.where(above <= 0, p_r[here], 0.0)
                        f_cols.append(jnp.where(above >= 0, weight, 0.0).astype(bf16))
                        r_cols.append(jnp.where(above <= 0, weight, 0.0).astype(bf16))
                    self.dscore[s, t, here[1]] += decay * picked
                f_rows.append(jnp.concatenate(f_cols, axis=1))
                r_rows.append(jnp.concatenate(r_cols, axis=1))
            self.y[s, 0, :, lanes_of(h)] = dot(jnp.concatenate(f_rows, axis=0), d_f)
            self.y[s, 1, :, lanes_of(h)] = dot(jnp.concatenate(r_rows, axis=0), d_r)

    def finish_grads(self, s):
        length, heads, state = self.length, self.heads, self.state
        b_m, c_m = self.bc[s, 0, :, :state], self.bc[s, 1, :, :state]
        lane_row = iota2((1, LANES), 1)
        total = jnp.zeros((1, LANES), f32)
        ends = jnp.exp(self.end_row[s])
        inward = [self.states(1, s, d) for d in range(2)]
        carried = [dot(b_m, inward[d]) for d in range(2)]
        for r, t in self.strips():
            for h in range(heads):
                x = self.x[s, t, lanes_of(h)].astype(f32)
                skipped = self.dy[s, 0, t, lanes_of(h)].astype(f32) + self.dy[s, 1, t, lanes_of(h)].astype(f32)
                dx = self.skip[:, h : h + 1] * skipped
                for d in range(2):
                    here = carried[d][r : r + STRIP, h * LANES : (h + 1) * LANES]
                    u = self.y[s, d, t, lanes_of(h)] + self.wide[s, d, t, lanes_of(h)] * here
                    dx += u
                    self.prod[s, d, t, lanes_of(h)] = (x * u).astype(bf16)
                self.dx[pl.ds(s * length + r, STRIP), lanes_of(h)] = dx.astype(bf16)
        d_b = dot(self.tailed[s, 0], inward[0], NT) + dot(self.tailed[s, 1], inward[1], NT)
        for h in range(heads):
            s_f, s_r = (self.take_rows(self.fin, 0, s, h, d).astype(f32) for d in range(2))
            a_f, a_r = (self.take_rows(self.fin, 1, s, h, d).astype(f32) for d in range(2))
            own, own_r = (self.take_rows(self.par, d, s, h, d).astype(f32) for d in range(2))
            decay = ends[:, h : h + 1]
            ending = a_f * (decay * s_f + own) + s_r * (decay * a_r + own_r)
            ended = jnp.sum(jnp.sum(ending, axis=0, keepdims=True), axis=1, keepdims=True)
            total = jnp.where(lane_row == h, ended, total)
        into_f, into_r = (dot(self.prod[s, d], self.gather[...]) for d in range(2))
        d_cum = self.cols[0, s] - into_f
        d_exc = into_r - self.cols[1, s]
        upper = (iota2((length, length), 0) <= iota2((length, length), 1)).astype(bf16)
        d_la = exact_dot(upper, d_cum + d_exc, heads) - d_exc + total
        d_raw = (into_f + into_r) * self.keep[1, s] - self.keep[0, s] * d_la
        d_raw = jnp.where(iota2((length, LANES), 1) < heads, d_raw, 0.0)
        scores = self.dscore[s].astype(bf16)
        d_b += dot(scores, c_m)
        d_c = self.carried[s, :, :state] + dot(scores, b_m, TN)
        tail = jnp.concatenate([d_raw[:, : LANES - 2 * state], d_b, d_c], axis=1)
        self.tail[pl.ds(s * length, length)] = tail.astype(bf16)

    def half(self, which, k, away):
        length = self.length
        lower, upper = k * CHUNK, self.width - CHUNK - k * CHUNK
        here = jnp.where(self.mine == (1 if away else 0), lower, upper)
        there = lower + upper - here

        def product(s, start):
            at, rows = chunk_at(start), pl.ds(s * length, length)
            if which == 0:
                return dot(self.z[rows], self.wo[:, at])
            return dot(self.dx[rows], self.wv[at, :], NT) + dot(self.tail[rows], self.side[:, at])

        return product(0, here) + dot(product(1, there).astype(bf16), mirror_matrix())

    def send(self, which, k):
        snd = self.out_snd if which == 0 else self.dh_snd
        snd[k] = self.half(which, k, True).astype(bf16)
        self.mp_copy(which, k).start()

    def settle(self, which, k, kept):
        rcv, out = (self.out_rcv, self.out) if which == 0 else (self.dh_rcv, self.dh)
        self.mp_copy(which, k).wait()
        at = jnp.where(self.mine == 0, k, self.chunks - 1 - k)
        out[:, chunk_at(at * CHUNK)] = (kept + rcv[k].astype(f32)).astype(bf16)


def layer_kernel(sizes, *refs):
    layer = Layer(sizes, refs + (pltpu.get_barrier_semaphore(),))
    length, inner = layer.length, layer.inner
    hidden_load, value_load, cot_load, out_load = layer.loads()
    small_loads = layer.small_loads()
    for load in [hidden_load] + small_loads + [value_load, cot_load, out_load]:
        load.start()
    layer.greet()
    layer.constants()
    for load in small_loads:
        load.wait()
    layer.side_weights()
    hidden_load.wait()
    layer.flip_into(layer.src)
    layer.prepare()
    for s in range(2):
        layer.end_row[s] = layer.cols[0, s, length - 1 : length]
    layer.meet()
    for copy in layer.near_decays() + layer.far_decays():
        copy.start()
    value_load.wait()

    def values(s):
        def one(k, none):
            at = chunk_at(k * CHUNK)
            layer.x[s, :, at] = dot(layer.src[pl.ds(s * length, length)], layer.wv[:, at]).astype(bf16)
            return none

        lax.fori_loop(0, inner // CHUNK, one, 0)

    def output_grads(k, none):
        at = chunk_at(k * CHUNK)
        both = dot(layer.grd[...], layer.wo[at, :], NT)
        for s in range(2):
            dz = jnp.where(known, both[s * length : (s + 1) * length], 0.0).astype(bf16)
            layer.g[s, :, at] = dz.astype(f32) * layer.gain[:, at]
        return none

    for s in range(2):
        values(s)
        layer.ends(s)
        layer.begin(0, s)
    layer.take_near()
    layer.spread(0, 0)
    cot_load.wait()
    layer.flip_into(layer.grd)
    known = jnp.where(layer.ids[...] != 4, 1.0, 0.0)
    known = jnp.broadcast_to(known, (8, length)).T[:, :1] > 0.5
    out_load.wait()
    middle = inner // CHUNK // 2
    lax.fori_loop(0, middle, output_grads, 0)
    layer.spread(0, 1)
    lax.fori_loop(middle, inner // CHUNK, output_grads, 0)
    layer.take_far()
    layer.send_home(0, 0)
    layer.local_outputs(0)
    layer.send_home(0, 1)
    layer.local_outputs(1)
    layer.arrive(0, 0)
    layer.finish_outputs(0)
    layer.begin(1, 0)
    layer.arrive(0, 1)
    layer.finish_outputs(1)
    layer.begin(1, 1)
    chunks = range(layer.chunks)
    layer.between(0)
    layer.spread(1, 0)
    layer.send(0, 0)
    layer.send(0, 1)
    layer.spread(1, 1)
    layer.send(0, 2)
    layer.send(0, 3)
    layer.send_home(1, 0)
    layer.local_grads(0)
    layer.between(1)
    layer.send_home(1, 1)
    layer.local_grads(1)
    layer.arrive(1, 0)
    layer.finish_grads(0)
    layer.arrive(1, 1)
    layer.finish_grads(1)
    for k in chunks:
        layer.send(1, k)
    for k in chunks:
        layer.settle(0, k, layer.half(0, k, False))
    for k in chunks:
        layer.hold[k] = layer.half(1, k, False)
    for k in chunks:
        layer.settle(1, k, layer.hold[k])


def per_device(
    hidden, ids, w_value, w_bc, w_step, step_bias, decay_log, skip, norm_gain, w_out, cotangent
):
    length, width = hidden.shape
    heads, inner, state = w_step.shape[1], w_value.shape[1], w_bc.shape[2] // 2
    count, parts = lax.axis_size("seq"), lax.axis_size("mp")
    assert w_bc.shape[1] == 1 and inner == heads * LANES
    group = 1
    while 4 * group * group <= count:
        group *= 2
    assert count % group == 0 and heads % group == 0 and parts == 2
    planes, each = count // group, heads // group
    rows = each * state
    share = width // parts
    chunks = share // CHUNK
    vmem, hbm = pl.BlockSpec(memory_space=pltpu.VMEM), pl.BlockSpec(memory_space=pltpu.HBM)
    parcel = (2, 2, group, 2, rows, LANES)
    travel = (chunks, length, CHUNK)
    sem = pltpu.SemaphoreType.DMA
    scratch = [
        pltpu.VMEM((2 * length, width), bf16),
        pltpu.VMEM((2 * length, width), bf16),
        pltpu.VMEM(w_value.shape, bf16),
        pltpu.VMEM(w_out.shape, bf16),
        pltpu.VMEM((LANES, width), bf16),
        pltpu.VMEM((2, length, inner), bf16),
        pltpu.VMEM((2, length, inner), f32),
        pltpu.VMEM((2, length, inner), f32),
        pltpu.VMEM((2, 2, length, inner), f32),
        pltpu.VMEM((2, 2, length, inner), bf16),
        pltpu.VMEM((2, 2, length, inner), bf16),
        pltpu.VMEM((2, 2, length, inner), bf16),
        pltpu.VMEM((LANES, inner), bf16),
        pltpu.VMEM((inner, LANES), bf16),
        pltpu.VMEM((2, 2, length, inner), f32),
        pltpu.VMEM((2 * length, inner), bf16),
        pltpu.VMEM((2, 2, length, inner), bf16),
        pltpu.VMEM((2 * length, inner), bf16),
        pltpu.VMEM((2 * length, LANES), bf16),
        pltpu.VMEM((2, length, LANES), f32),
        pltpu.VMEM((len(COLUMNS), 2, length, LANES), f32),
        pltpu.VMEM((len(COLUMNS), 2, heads, length), f32),
        pltpu.VMEM((2, 2, length, LANES), bf16),
        pltpu.VMEM((length, length), f32),
        pltpu.VMEM((2, length, length), f32),
        pltpu.VMEM((2, length, LANES), f32),
        pltpu.VMEM((2, 2 * state, length), f32),
        pltpu.VMEM((2, 2, length, LANES), f32),
        pltpu.VMEM((2, 1, LANES), f32),
        pltpu.VMEM((1, LANES), f32),
        pltpu.VMEM((count, 1, LANES), f32),
        pltpu.VMEM((2, each, group, LANES), f32),
        pltpu.VMEM((2, each, planes, LANES), f32),
        pltpu.VMEM(parcel, bf16),
        pltpu.VMEM(parcel, bf16),
        pltpu.VMEM((2, 2, 2, rows, LANES), bf16),
        pltpu.VMEM((2, 2, planes, rows, LANES), bf16),
        pltpu.VMEM(parcel, bf16),
        pltpu.VMEM(parcel, bf16),
        pltpu.VMEM(travel, bf16),
        pltpu.VMEM(travel, bf16),
        pltpu.VMEM(travel, bf16),
        pltpu.VMEM(travel, bf16),
        pltpu.VMEM(travel, f32),
        sem((4,)),
        sem((2, planes, group)),
        sem((2, 4, group)),
        sem((2, 4, planes)),
        sem((2, 4, group)),
        sem((2, 2, chunks)),
        sem((7,)),
        pltpu.VMEM((1, length), jnp.int32),
        pltpu.VMEM((heads, width), bf16),
        pltpu.VMEM((2 * state, width), bf16),
        pltpu.VMEM((1, heads), f32),
        pltpu.VMEM((1, heads), f32),
        pltpu.VMEM((1, heads), f32),
        pltpu.VMEM((1, inner), f32),
    ]
    sizes = (length, width, inner, heads, state, count, group, parts)
    return pl.pallas_call(
        partial(layer_kernel, sizes),
        in_specs=[hbm] * 11,
        out_specs=(vmem, vmem),
        out_shape=(jax.ShapeDtypeStruct((length, share), bf16),) * 2,
        scratch_shapes=scratch,
        compiler_params=pltpu.CompilerParams(
            collective_id=0, has_side_effects=True, vmem_limit_bytes=52 * 1024 * 1024
        ),
    )(
        *(
            pltpu.with_memory_space_constraint(value, pltpu.HBM)
            for value in (
                hidden, cotangent, w_value, w_out, ids[None], w_step.T, w_bc.reshape(width, -1).T,
                step_bias[None], decay_log[None], skip[None], norm_gain[None],
            )
        )
    )


def solution(mesh):
    in_specs = (
        P("seq", None),
        P("seq"),
        P(None, "mp"),
        P(None, "mp", None),
        P(None, "mp"),
        P("mp"),
        P("mp"),
        P("mp"),
        P("mp"),
        P("mp", None),
        P("seq", None),
    )
    out_specs = (P("seq", "mp"), P("seq", "mp"))
    return jax.shard_map(
        per_device, mesh=mesh, in_specs=in_specs, out_specs=out_specs, check_vma=False
    )
```

```python
from functools import partial

import jax
import jax.numpy as jnp
from jax import lax
from jax.experimental import pallas as pl
from jax.experimental.pallas import tpu as pltpu
from jax.sharding import PartitionSpec as P

f32, bf16 = jnp.float32, jnp.bfloat16
epsilon = 1e-05
LANES = 128
CHUNK = 256
STRIP = 32
NN = (((1,), (0,)), ((), ()))
NT = (((1,), (1,)), ((), ()))
TN = (((0,), (0,)), ((), ()))
MESH_ID = pl.DeviceIdType.MESH
COLUMNS = ("cum", "exc", "low", "high", "grow_f", "grow_r", "tail_f", "tail_r")

NAMES = (
    "hidden_hbm", "cot_hbm", "wv_hbm", "wo_hbm", "ids_hbm", "step_hbm", "bc_hbm", "bias_hbm",
    "decay_hbm", "skip_hbm", "gain_hbm", "out", "dh", "src", "grd", "wv", "wo", "side", "x", "g", "direct", "wide", "grown",
    "tailed", "prod", "pick", "gather", "y", "z", "dy", "dx", "tail", "aux", "cols", "rows", "bc",
    "scores", "dscore", "carried", "bct", "keep", "end_row", "dec_row", "dec_got", "dec", "plane_dec",
    "par", "got", "agg", "far", "back", "fin", "out_snd", "out_rcv", "dh_snd", "dh_rcv", "hold",
    "load_sem", "dec_sem", "go_sem", "far_sem", "home_sem", "mp_sem", "small_sem", "ids", "step_t", "bc_t", "bias",
    "decay", "skip", "gain", "barrier",
)


def dot(a, b, dims=NN):
    return lax.dot_general(a, b, dims, preferred_element_type=f32)


def iota2(shape, axis):
    return lax.broadcasted_iota(jnp.int32, shape, axis)


def mirror_matrix():
    return (iota2((CHUNK, CHUNK), 0) + iota2((CHUNK, CHUNK), 1) == CHUNK - 1).astype(bf16)


def chunk_at(start):
    return pl.ds(pl.multiple_of(start, CHUNK), CHUNK)


def lanes_of(h):
    return pl.ds(h * LANES, LANES)


def thirds(value, used):
    value = jnp.where(iota2(value.shape, 1) < used, value, 0.0)
    hi = value.astype(bf16).astype(f32)
    rest = value - hi
    mid = rest.astype(bf16).astype(f32)
    low = (rest - mid).astype(bf16).astype(f32)
    return (hi + pltpu.roll(mid, used, 1) + pltpu.roll(low, 2 * used, 1)).astype(bf16)


def exact_dot(matrix, value, used):
    result = dot(matrix, thirds(value, used))
    result += pltpu.roll(result, LANES - used, 1) + pltpu.roll(result, LANES - 2 * used, 1)
    return jnp.where(iota2(value.shape, 1) < used, result, 0.0)


class Layer:
    def __init__(self, sizes, refs):
        self.length, self.width, self.inner, self.heads, self.state, self.count, self.group, self.parts = sizes
        for name, ref in zip(NAMES, refs):
            setattr(self, name, ref)
        self.planes = self.count // self.group
        self.each = self.heads // self.group
        me = lax.axis_index("seq")
        self.me, self.plane, self.member = me, me // self.group, lax.rem(me, self.group)
        self.mine = lax.axis_index("mp")
        self.share = self.width // self.parts
        self.chunks = self.share // CHUNK

    def loads(self):
        top = self.src.at[pl.ds(0, self.length)]
        bottom = self.grd.at[pl.ds(0, self.length)]
        pairs = [(self.hidden_hbm, top), (self.wv_hbm, self.wv), (self.cot_hbm, bottom), (self.wo_hbm, self.wo)]
        return [pltpu.make_async_copy(a, b, self.load_sem.at[i]) for i, (a, b) in enumerate(pairs)]

    def small_loads(self):
        pairs = [
            (self.step_hbm, self.step_t), (self.bc_hbm, self.bc_t), (self.bias_hbm, self.bias),
            (self.decay_hbm, self.decay), (self.skip_hbm, self.skip), (self.gain_hbm, self.gain), (self.ids_hbm, self.ids),
        ]
        return [pltpu.make_async_copy(a, b, self.small_sem.at[i]) for i, (a, b) in enumerate(pairs)]

    def peer(self, hop):
        return lax.rem(self.me + hop, self.count)

    def greet(self):
        def one(hop, none):
            pl.semaphore_signal(self.barrier, inc=1, device_id={"seq": self.peer(hop)}, device_id_type=MESH_ID)
            return none

        lax.fori_loop(1, self.count, one, 0)
        pl.semaphore_signal(self.barrier, inc=1, device_id={"mp": 1 - self.mine}, device_id_type=MESH_ID)

    def meet(self):
        pl.semaphore_wait(self.barrier, self.count)

    def remote(self, src, dst, sems, where, device):
        return pltpu.make_async_remote_copy(
            src_ref=src, dst_ref=dst, send_sem=sems.at[(0,) + where], recv_sem=sems.at[(1,) + where],
            device_id=device, device_id_type=MESH_ID,
        )

    def decay_copy(self, plane_hop, member_hop):
        plane = lax.rem(self.plane + plane_hop, self.planes)
        to = plane * self.group + lax.rem(self.member + member_hop, self.group)
        return self.remote(self.dec_row, self.dec_got.at[self.me], self.dec_sem, (plane_hop, member_hop), {"seq": to})

    def near_decays(self):
        return [self.decay_copy(0, m) for m in range(1, self.group)]

    def far_decays(self):
        return [self.decay_copy(p, m) for p in range(1, self.planes) for m in range(self.group)]

    def gather_copies(self, e, s):
        for hop in range(1, self.group):
            to = lax.rem(self.member + hop, self.group)
            yield self.remote(
                self.par.at[e, s, to], self.got.at[e, s, self.member], self.go_sem, (2 * e + s, hop),
                {"seq": self.plane * self.group + to},
            )

    def plane_copies(self, e, s):
        for hop in range(1, self.planes):
            to = lax.rem(self.plane + hop, self.planes)
            which = jnp.where(to > self.plane, e, 1 - e)
            yield self.remote(
                self.agg.at[e, s, which], self.far.at[e, s, self.plane], self.far_sem, (2 * e + s, hop),
                {"seq": to * self.group + self.member},
            )

    def home_copies(self, e, s):
        for hop in range(1, self.group):
            to = lax.rem(self.member + hop, self.group)
            yield self.remote(
                self.back.at[e, s, to], self.fin.at[e, s, self.member], self.home_sem, (2 * e + s, hop),
                {"seq": self.plane * self.group + to},
            )

    def mp_copy(self, which, k):
        snd, rcv = (self.out_snd, self.out_rcv) if which == 0 else (self.dh_snd, self.dh_rcv)
        return self.remote(snd.at[k], rcv.at[k], self.mp_sem, (which, k), {"mp": 1 - self.mine})

    def put_rows(self, e, s, h, which, value):
        at = pl.ds(h % self.each * self.state, self.state)
        self.par[e, s, h // self.each, which, at] = value.astype(bf16)

    def take_rows(self, ref, e, s, h, which):
        return ref[e, s, h // self.each, which, pl.ds(h % self.each * self.state, self.state)]

    def decays_of(self, rows, s, q):
        table = jnp.concatenate(rows, axis=0)
        head = s * self.heads + self.member * self.each + q
        picked = jnp.sum(jnp.where(iota2(table.shape, 1) == head, table, 0.0), axis=1, keepdims=True)
        return jnp.broadcast_to(picked, table.shape)

    def take_near(self):
        for copy in self.near_decays():
            copy.wait()
        self.dec_got[self.me] = self.dec_row[...]
        rows = [self.dec_got[self.plane * self.group + m] for m in range(self.group)]
        for s in range(2):
            for q in range(self.each):
                self.dec[s, q] = self.decays_of(rows, s, q)

    def take_far(self):
        for copy in self.far_decays():
            copy.wait()
        rows = [self.dec_got[j] for j in range(self.count)]
        for s in range(2):
            for q in range(self.each):
                wide = self.decays_of(rows, s, q)
                for p in range(self.planes):
                    product = wide[p * self.group : p * self.group + 1]
                    for m in range(1, self.group):
                        product = product * wide[p * self.group + m : p * self.group + m + 1]
                    self.plane_dec[s, q, p : p + 1] = product

    def members(self, e, s, which, q, total, visit):
        order = range(self.group) if which == e else range(self.group - 1, -1, -1)
        at = pl.ds(q * self.state, self.state)
        for m in order:
            visit(m, at, total)
            total = self.dec[s, q, m : m + 1] * total + self.got[e, s, m, which, at].astype(f32)
        return total

    def begin(self, e, s):
        for copy in self.gather_copies(e, s):
            copy.start()

    def spread(self, e, s):
        for copy in self.gather_copies(e, s):
            copy.wait()
        self.got[e, s, self.member] = self.par[e, s, self.member]
        self.far[e, s, self.plane] = jnp.zeros((self.each * self.state, LANES), bf16)
        for which in range(2):
            for q in range(self.each):
                total = self.members(e, s, which, q, jnp.zeros((self.state, LANES), f32), lambda m, at, total: None)
                self.agg[e, s, which, pl.ds(q * self.state, self.state)] = total.astype(bf16)
        for copy in self.plane_copies(e, s):
            copy.start()

    def send_home(self, e, s):
        for copy in self.plane_copies(e, s):
            copy.wait()
        for which in range(2):
            rising = which == e
            for q in range(self.each):
                total = jnp.zeros((self.state, LANES), f32)
                for p in range(self.planes) if rising else range(self.planes - 1, -1, -1):
                    got = self.far[e, s, p, pl.ds(q * self.state, self.state)].astype(f32)
                    longer = self.plane_dec[s, q, p : p + 1] * total + got
                    total = jnp.where(p < self.plane if rising else p > self.plane, longer, total)

                def keep(m, at, value):
                    self.back[e, s, m, which, at] = value.astype(bf16)

                self.members(e, s, which, q, total, keep)
        for copy in self.home_copies(e, s):
            copy.start()

    def arrive(self, e, s):
        for copy in self.home_copies(e, s):
            copy.wait()
        self.fin[e, s, self.member] = self.back[e, s, self.member]

    def flip_into(self, ref):
        mirror = mirror_matrix()
        for k in range(self.width // CHUNK):
            tile = ref[pl.ds(0, self.length), pl.ds(k * CHUNK, CHUNK)]
            there = pl.ds(self.width - CHUNK - k * CHUNK, CHUNK)
            ref[pl.ds(self.length, self.length), there] = dot(tile, mirror).astype(bf16)

    def constants(self):
        across = iota2((LANES, self.inner), 0), iota2((LANES, self.inner), 1) // LANES
        match = lax.rem(across[0], self.heads) == across[1]
        self.pick[...] = jnp.where(match & (across[0] < 3 * self.heads), 1.0, 0.0).astype(bf16)
        down = iota2((self.inner, LANES), 0) // LANES, iota2((self.inner, LANES), 1)
        self.gather[...] = (down[0] == down[1]).astype(bf16)

    def side_weights(self):
        gap = LANES - self.heads - 2 * self.state
        self.side[...] = jnp.concatenate(
            [self.step_t[...].astype(f32), jnp.zeros((gap, self.width), f32), self.bc_t[...].astype(f32)], axis=0
        ).astype(bf16)

    def prepare(self):
        length, heads, state, used = self.length, self.heads, self.state, 2 * self.heads
        shape = (length, LANES)
        lane = iota2(shape, 1)
        aux = dot(self.src[...], self.side[...], NT)
        self.aux[0], self.aux[1] = aux[:length], aux[length:]
        raw = jnp.where(lane < heads, aux[:length], pltpu.roll(aux[length:], heads, 1))
        spare = jnp.zeros((1, LANES - used), f32)
        bias = jnp.concatenate([self.bias[...], self.bias[...], spare], axis=1)
        rate = jnp.exp(jnp.concatenate([self.decay[...], self.decay[...], spare], axis=1))
        shifted = jnp.where(lane < used, raw + bias, 0.0)
        dt = jnp.maximum(shifted, 0.0) + jnp.log1p(jnp.exp(-jnp.abs(shifted)))
        la = jnp.where(lane < used, -rate * dt, 0.0)
        lower = (iota2((length, length), 0) >= iota2((length, length), 1)).astype(bf16)
        cum = exact_dot(lower, la, used)
        exc = cum - la
        end = cum[length - 1 : length]
        log_dt = jnp.log(jnp.maximum(dt, 1e-38))
        grow_f, grow_r = jnp.exp(cum), jnp.exp(end - exc)
        tail_f, tail_r = dt * jnp.exp(end - cum), dt * jnp.exp(exc)
        values = (cum, exc, cum - log_dt, exc + log_dt, grow_f, grow_r, tail_f, tail_r)
        for i, value in enumerate(values):
            self.cols[i, 0] = value
            self.cols[i, 1] = pltpu.roll(value, LANES - heads, 1)
            flat = value.T
            self.rows[i, 0], self.rows[i, 1] = flat[:heads], flat[heads:used]
        sig = jax.nn.sigmoid(shifted)
        ratio = jnp.where(shifted < -15.0, 1.0, sig / jnp.maximum(dt, 1e-38))
        for i, value in ((0, sig * rate), (1, ratio)):
            self.keep[i, 0] = value
            self.keep[i, 1] = pltpu.roll(value, LANES - heads, 1)
        self.dec_row[...] = jnp.exp(end)
        for s in range(2):
            rounded = self.aux[s].astype(bf16)
            b_m, c_m = rounded[:, LANES - 2 * state : LANES - state], rounded[:, LANES - state :]
            self.bc[s, 0, :, :state] = b_m
            self.bc[s, 1, :, :state] = c_m
            self.bct[s] = rounded.astype(f32).T[LANES - 2 * state :]

    def row(self, name, s, h):
        return self.rows[COLUMNS.index(name), s, pl.ds(h, 1)]

    def col(self, name, s, h, at):
        return self.cols[COLUMNS.index(name), s, at, h : h + 1]

    def ends(self, s):
        b_t = self.bct[s, : self.state]
        for h in range(self.heads):
            left = jnp.concatenate([b_t * self.row("tail_f", s, h), b_t * self.row("tail_r", s, h)], axis=0).astype(bf16)
            both = dot(left, self.x[s, :, lanes_of(h)])
            self.put_rows(0, s, h, 0, both[: self.state])
            self.put_rows(0, s, h, 1, both[self.state :])

    def blocks(self):
        return [pl.ds(k * LANES, LANES) for k in range(self.length // LANES)]

    def local_outputs(self, s):
        at, state = self.blocks(), self.state
        b_m, c_m = self.bc[s, 0, :, :state], self.bc[s, 1, :, :state]
        self.scores[...] = dot(c_m, b_m, NT)
        below = iota2((LANES, LANES), 0) - iota2((LANES, LANES), 1)
        none = jnp.zeros((LANES, LANES), bf16)
        for h in range(self.heads):
            low_rows, high_rows = [], []
            for i, t in enumerate(at):
                cum, exc = self.col("cum", s, h, t), self.col("exc", s, h, t)
                low_cols, high_cols = [], []
                for j in range(len(at)):
                    cut = slice(j * LANES, (j + 1) * LANES)
                    to_f = lambda: cum - self.row("low", s, h)[:, cut]
                    to_r = lambda: self.row("high", s, h)[:, cut] - exc
                    power = to_f() if i > j else to_r() if i < j else jnp.minimum(to_f(), to_r())
                    mix = jnp.exp(power) * self.scores[t, cut]
                    low_cols.append(none if i < j else mix.astype(bf16) if i > j else jnp.where(below >= 0, mix, 0.0).astype(bf16))
                    high_cols.append(none if i > j else mix.astype(bf16) if i < j else jnp.where(below <= 0, mix, 0.0).astype(bf16))
                low_rows.append(jnp.concatenate(low_cols, axis=1))
                high_rows.append(jnp.concatenate(high_cols, axis=1))
            both = dot(jnp.concatenate(low_rows + high_rows, axis=0), self.x[s, :, lanes_of(h)])
            direct = self.skip[:, h : h + 1] * self.x[s, :, lanes_of(h)].astype(f32)
            self.direct[s, :, lanes_of(h)] = direct
            self.y[s, 0, :, lanes_of(h)] = both[: self.length] + direct
            self.y[s, 1, :, lanes_of(h)] = both[self.length :] + direct
        for d, name in ((0, "grow_f"), (1, "grow_r")):
            self.widen(name, s, d)

    def widen(self, name, s, d):
        self.wide[s, d] = dot(thirds(self.cols[COLUMNS.index(name), s], self.heads), self.pick[...])

    def strips(self):
        return [(r, pl.ds(r, STRIP)) for r in range(0, self.length, STRIP)]

    def states(self, e, s, d):
        return jnp.concatenate([self.take_rows(self.fin, e, s, h, d) for h in range(self.heads)], axis=1)

    def finish_outputs(self, s):
        length, heads, state = self.length, self.heads, self.state
        c_m = self.bc[s, 1, :, :state]
        carried = [dot(c_m, self.states(0, s, d)) for d in range(2)]
        zero = jnp.zeros((STRIP, LANES), f32)
        share = 1.0 / (heads * LANES)
        factors = []
        for r, t in self.strips():
            squares, pulls = [zero, zero], [zero, zero]
            for h in range(heads):
                g = self.g[s, t, lanes_of(h)]
                for d in range(2):
                    here = carried[d][r : r + STRIP, h * LANES : (h + 1) * LANES]
                    y = self.y[s, d, t, lanes_of(h)] + self.wide[s, d, t, lanes_of(h)] * here
                    self.y[s, d, t, lanes_of(h)] = y
                    squares[d] += y * y
                    pulls[d] += g * y
            scale = [lax.rsqrt(jnp.sum(q, axis=1, keepdims=True) * share + epsilon) for q in squares]
            means = [scale[d] * jnp.sum(pulls[d], axis=1, keepdims=True) * share for d in range(2)]
            factors.append((scale, [scale[d] * scale[d] * means[d] for d in range(2)]))
        for (r, t), (scale, pull) in zip(self.strips(), factors):
            for h in range(heads):
                g = self.g[s, t, lanes_of(h)]
                direct = self.direct[s, t, lanes_of(h)]
                y = [self.y[s, d, t, lanes_of(h)] for d in range(2)]
                z = (y[0] * scale[0] + y[1] * scale[1]) * self.gain[:, lanes_of(h)]
                self.z[pl.ds(s * length + r, STRIP), lanes_of(h)] = z.astype(bf16)
                for d in range(2):
                    grad = (scale[d] * g - pull[d] * y[d]).astype(bf16)
                    self.dy[s, d, t, lanes_of(h)] = grad
                    grad = grad.astype(f32)
                    self.grown[s, d, t, lanes_of(h)] = (self.wide[s, d, t, lanes_of(h)] * grad).astype(bf16)
                    self.prod[s, d, t, lanes_of(h)] = (grad * (y[d] - direct)).astype(bf16)
        c_t = self.bct[s, state:].astype(bf16)
        for d in range(2):
            own = dot(c_t, self.grown[s, d])
            for h in range(heads):
                self.put_rows(1, s, h, d, own[:, h * LANES : (h + 1) * LANES])

    def between(self, s):
        for d, name in ((0, "tail_f"), (1, "tail_r")):
            self.cols[d, s] = dot(self.prod[s, d], self.gather[...])
            self.widen(name, s, d)
            self.tailed[s, d] = (self.wide[s, d] * self.x[s].astype(f32)).astype(bf16)
        carried = [dot(self.grown[s, d], self.states(0, s, d), NT) for d in range(2)]
        self.carried[s, :, : self.state] = carried[0] + carried[1]

    def local_grads(self, s):
        at, state = self.blocks(), self.state
        b_m, c_m = self.bc[s, 0, :, :state], self.bc[s, 1, :, :state]
        self.scores[...] = dot(b_m, c_m, NT)
        self.dscore[s] = jnp.zeros_like(self.scores)
        above = iota2((LANES, LANES), 1) - iota2((LANES, LANES), 0)
        none = jnp.zeros((LANES, LANES), bf16)
        for h in range(self.heads):
            x_h = self.x[s, :, lanes_of(h)]
            d_f, d_r = self.dy[s, 0, :, lanes_of(h)], self.dy[s, 1, :, lanes_of(h)]
            p_f, p_r = dot(x_h, d_f, NT), dot(x_h, d_r, NT)
            f_rows, r_rows = [], []
            for i, t in enumerate(at):
                low, high = self.col("low", s, h, t), self.col("high", s, h, t)
                f_cols, r_cols = [], []
                for j in range(len(at)):
                    here = slice(i * LANES, (i + 1) * LANES), slice(j * LANES, (j + 1) * LANES)
                    to_f = lambda: self.row("cum", s, h)[:, here[1]] - low
                    to_r = lambda: high - self.row("exc", s, h)[:, here[1]]
                    power = to_f() if i < j else to_r() if i > j else jnp.minimum(to_f(), to_r())
                    decay = jnp.exp(power)
                    weight = decay * self.scores[here]
                    if i < j:
                        picked = p_f[here]
                        f_cols.append(weight.astype(bf16))
                        r_cols.append(none)
                    elif i > j:
                        picked = p_r[here]
                        f_cols.append(none)
                        r_cols.append(weight.astype(bf16))
                    else:
                        picked = jnp.where(above >= 0, p_f[here], 0.0) + jnp.where(above <= 0, p_r[here], 0.0)
                        f_cols.append(jnp.where(above >= 0, weight, 0.0).astype(bf16))
                        r_cols.append(jnp.where(above <= 0, weight, 0.0).astype(bf16))
                    self.dscore[s, t, here[1]] += decay * picked
                f_rows.append(jnp.concatenate(f_cols, axis=1))
                r_rows.append(jnp.concatenate(r_cols, axis=1))
            self.y[s, 0, :, lanes_of(h)] = dot(jnp.concatenate(f_rows, axis=0), d_f)
            self.y[s, 1, :, lanes_of(h)] = dot(jnp.concatenate(r_rows, axis=0), d_r)

    def finish_grads(self, s):
        length, heads, state = self.length, self.heads, self.state
        b_m, c_m = self.bc[s, 0, :, :state], self.bc[s, 1, :, :state]
        lane_row = iota2((1, LANES), 1)
        total = jnp.zeros((1, LANES), f32)
        ends = jnp.exp(self.end_row[s])
        inward = [self.states(1, s, d) for d in range(2)]
        carried = [dot(b_m, inward[d]) for d in range(2)]
        for r, t in self.strips():
            for h in range(heads):
                x = self.x[s, t, lanes_of(h)].astype(f32)
                skipped = self.dy[s, 0, t, lanes_of(h)].astype(f32) + self.dy[s, 1, t, lanes_of(h)].astype(f32)
                dx = self.skip[:, h : h + 1] * skipped
                for d in range(2):
                    here = carried[d][r : r + STRIP, h * LANES : (h + 1) * LANES]
                    u = self.y[s, d, t, lanes_of(h)] + self.wide[s, d, t, lanes_of(h)] * here
                    dx += u
                    self.prod[s, d, t, lanes_of(h)] = (x * u).astype(bf16)
                self.dx[pl.ds(s * length + r, STRIP), lanes_of(h)] = dx.astype(bf16)
        d_b = dot(self.tailed[s, 0], inward[0], NT) + dot(self.tailed[s, 1], inward[1], NT)
        for h in range(heads):
            s_f, s_r = (self.take_rows(self.fin, 0, s, h, d).astype(f32) for d in range(2))
            a_f, a_r = (self.take_rows(self.fin, 1, s, h, d).astype(f32) for d in range(2))
            own, own_r = (self.take_rows(self.par, d, s, h, d).astype(f32) for d in range(2))
            decay = ends[:, h : h + 1]
            ending = a_f * (decay * s_f + own) + s_r * (decay * a_r + own_r)
            ended = jnp.sum(jnp.sum(ending, axis=0, keepdims=True), axis=1, keepdims=True)
            total = jnp.where(lane_row == h, ended, total)
        into_f, into_r = (dot(self.prod[s, d], self.gather[...]) for d in range(2))
        d_cum = self.cols[0, s] - into_f
        d_exc = into_r - self.cols[1, s]
        upper = (iota2((length, length), 0) <= iota2((length, length), 1)).astype(bf16)
        d_la = exact_dot(upper, d_cum + d_exc, heads) - d_exc + total
        d_raw = (into_f + into_r) * self.keep[1, s] - self.keep[0, s] * d_la
        d_raw = jnp.where(iota2((length, LANES), 1) < heads, d_raw, 0.0)
        scores = self.dscore[s].astype(bf16)
        d_b += dot(scores, c_m)
        d_c = self.carried[s, :, :state] + dot(scores, b_m, TN)
        tail = jnp.concatenate([d_raw[:, : LANES - 2 * state], d_b, d_c], axis=1)
        self.tail[pl.ds(s * length, length)] = tail.astype(bf16)

    def half(self, which, k, away):
        length = self.length
        lower, upper = k * CHUNK, self.width - CHUNK - k * CHUNK
        here = jnp.where(self.mine == (1 if away else 0), lower, upper)
        there = lower + upper - here

        def product(s, start):
            at, rows = chunk_at(start), pl.ds(s * length, length)
            if which == 0:
                return dot(self.z[rows], self.wo[:, at])
            return dot(self.dx[rows], self.wv[at, :], NT) + dot(self.tail[rows], self.side[:, at])

        return product(0, here) + dot(product(1, there).astype(bf16), mirror_matrix())

    def send(self, which, k):
        snd = self.out_snd if which == 0 else self.dh_snd
        snd[k] = self.half(which, k, True).astype(bf16)
        self.mp_copy(which, k).start()

    def settle(self, which, k, kept):
        rcv, out = (self.out_rcv, self.out) if which == 0 else (self.dh_rcv, self.dh)
        self.mp_copy(which, k).wait()
        at = jnp.where(self.mine == 0, k, self.chunks - 1 - k)
        out[:, chunk_at(at * CHUNK)] = (kept + rcv[k].astype(f32)).astype(bf16)


def layer_kernel(sizes, *refs):
    layer = Layer(sizes, refs + (pltpu.get_barrier_semaphore(),))
    length, inner = layer.length, layer.inner
    hidden_load, value_load, cot_load, out_load = layer.loads()
    small_loads = layer.small_loads()
    for load in [hidden_load] + small_loads + [value_load, cot_load, out_load]:
        load.start()
    layer.greet()
    layer.constants()
    for load in small_loads:
        load.wait()
    layer.side_weights()
    hidden_load.wait()
    layer.flip_into(layer.src)
    layer.prepare()
    for s in range(2):
        layer.end_row[s] = layer.cols[0, s, length - 1 : length]
    layer.meet()
    for copy in layer.near_decays() + layer.far_decays():
        copy.start()
    value_load.wait()

    def values(s):
        def one(k, none):
            at = chunk_at(k * CHUNK)
            layer.x[s, :, at] = dot(layer.src[pl.ds(s * length, length)], layer.wv[:, at]).astype(bf16)
            return none

        lax.fori_loop(0, inner // CHUNK, one, 0)

    def output_grads(k, none):
        at = chunk_at(k * CHUNK)
        both = dot(layer.grd[...], layer.wo[at, :], NT)
        for s in range(2):
            dz = jnp.where(known, both[s * length : (s + 1) * length], 0.0).astype(bf16)
            layer.g[s, :, at] = dz.astype(f32) * layer.gain[:, at]
        return none

    for s in range(2):
        values(s)
        layer.ends(s)
        layer.begin(0, s)
    layer.take_near()
    layer.spread(0, 0)
    cot_load.wait()
    layer.flip_into(layer.grd)
    known = jnp.where(layer.ids[...] != 4, 1.0, 0.0)
    known = jnp.broadcast_to(known, (8, length)).T[:, :1] > 0.5
    out_load.wait()
    middle = inner // CHUNK // 2
    lax.fori_loop(0, middle, output_grads, 0)
    layer.spread(0, 1)
    lax.fori_loop(middle, inner // CHUNK, output_grads, 0)
    layer.take_far()
    layer.send_home(0, 0)
    layer.local_outputs(0)
    layer.send_home(0, 1)
    layer.local_outputs(1)
    layer.arrive(0, 0)
    layer.finish_outputs(0)
    layer.begin(1, 0)
    layer.arrive(0, 1)
    layer.finish_outputs(1)
    layer.begin(1, 1)
    chunks = range(layer.chunks)
    layer.between(0)
    layer.spread(1, 0)
    for k in chunks[: layer.chunks // 2]:
        layer.send(0, k)
    layer.spread(1, 1)
    for k in chunks[layer.chunks // 2 :]:
        layer.send(0, k)
    layer.send_home(1, 0)
    layer.local_grads(0)
    layer.between(1)
    layer.send_home(1, 1)
    layer.local_grads(1)
    layer.arrive(1, 0)
    layer.finish_grads(0)
    layer.arrive(1, 1)
    layer.finish_grads(1)
    for k in chunks:
        layer.send(1, k)
    for k in chunks:
        layer.settle(0, k, layer.half(0, k, False))
    for k in chunks:
        layer.hold[k] = layer.half(1, k, False)
    for k in chunks:
        layer.settle(1, k, layer.hold[k])


def per_device(
    hidden, ids, w_value, w_bc, w_step, step_bias, decay_log, skip, norm_gain, w_out, cotangent
):
    length, width = hidden.shape
    heads, inner, state = w_step.shape[1], w_value.shape[1], w_bc.shape[2] // 2
    count, parts = lax.axis_size("seq"), lax.axis_size("mp")
    assert w_bc.shape[1] == 1 and inner == heads * LANES
    group = 1
    while 4 * group * group <= count:
        group *= 2
    assert count % group == 0 and heads % group == 0 and parts == 2
    planes, each = count // group, heads // group
    rows = each * state
    share = width // parts
    chunks = share // CHUNK
    vmem, hbm = pl.BlockSpec(memory_space=pltpu.VMEM), pl.BlockSpec(memory_space=pltpu.HBM)
    parcel = (2, 2, group, 2, rows, LANES)
    travel = (chunks, length, CHUNK)
    sem = pltpu.SemaphoreType.DMA
    scratch = [
        pltpu.VMEM((2 * length, width), bf16),
        pltpu.VMEM((2 * length, width), bf16),
        pltpu.VMEM(w_value.shape, bf16),
        pltpu.VMEM(w_out.shape, bf16),
        pltpu.VMEM((LANES, width), bf16),
        pltpu.VMEM((2, length, inner), bf16),
        pltpu.VMEM((2, length, inner), f32),
        pltpu.VMEM((2, length, inner), f32),
        pltpu.VMEM((2, 2, length, inner), f32),
        pltpu.VMEM((2, 2, length, inner), bf16),
        pltpu.VMEM((2, 2, length, inner), bf16),
        pltpu.VMEM((2, 2, length, inner), bf16),
        pltpu.VMEM((LANES, inner), bf16),
        pltpu.VMEM((inner, LANES), bf16),
        pltpu.VMEM((2, 2, length, inner), f32),
        pltpu.VMEM((2 * length, inner), bf16),
        pltpu.VMEM((2, 2, length, inner), bf16),
        pltpu.VMEM((2 * length, inner), bf16),
        pltpu.VMEM((2 * length, LANES), bf16),
        pltpu.VMEM((2, length, LANES), f32),
        pltpu.VMEM((len(COLUMNS), 2, length, LANES), f32),
        pltpu.VMEM((len(COLUMNS), 2, heads, length), f32),
        pltpu.VMEM((2, 2, length, LANES), bf16),
        pltpu.VMEM((length, length), f32),
        pltpu.VMEM((2, length, length), f32),
        pltpu.VMEM((2, length, LANES), f32),
        pltpu.VMEM((2, 2 * state, length), f32),
        pltpu.VMEM((2, 2, length, LANES), f32),
        pltpu.VMEM((2, 1, LANES), f32),
        pltpu.VMEM((1, LANES), f32),
        pltpu.VMEM((count, 1, LANES), f32),
        pltpu.VMEM((2, each, group, LANES), f32),
        pltpu.VMEM((2, each, planes, LANES), f32),
        pltpu.VMEM(parcel, bf16),
        pltpu.VMEM(parcel, bf16),
        pltpu.VMEM((2, 2, 2, rows, LANES), bf16),
        pltpu.VMEM((2, 2, planes, rows, LANES), bf16),
        pltpu.VMEM(parcel, bf16),
        pltpu.VMEM(parcel, bf16),
        pltpu.VMEM(travel, bf16),
        pltpu.VMEM(travel, bf16),
        pltpu.VMEM(travel, bf16),
        pltpu.VMEM(travel, bf16),
        pltpu.VMEM(travel, f32),
        sem((4,)),
        sem((2, planes, group)),
        sem((2, 4, group)),
        sem((2, 4, planes)),
        sem((2, 4, group)),
        sem((2, 2, chunks)),
        sem((7,)),
        pltpu.VMEM((1, length), jnp.int32),
        pltpu.VMEM((heads, width), bf16),
        pltpu.VMEM((2 * state, width), bf16),
        pltpu.VMEM((1, heads), f32),
        pltpu.VMEM((1, heads), f32),
        pltpu.VMEM((1, heads), f32),
        pltpu.VMEM((1, inner), f32),
    ]
    sizes = (length, width, inner, heads, state, count, group, parts)
    return pl.pallas_call(
        partial(layer_kernel, sizes),
        in_specs=[hbm] * 11,
        out_specs=(vmem, vmem),
        out_shape=(jax.ShapeDtypeStruct((length, share), bf16),) * 2,
        scratch_shapes=scratch,
        compiler_params=pltpu.CompilerParams(
            collective_id=0, has_side_effects=True, vmem_limit_bytes=52 * 1024 * 1024
        ),
    )(
        *(
            pltpu.with_memory_space_constraint(value, pltpu.HBM)
            for value in (
                hidden, cotangent, w_value, w_out, ids[None], w_step.T, w_bc.reshape(width, -1).T,
                step_bias[None], decay_log[None], skip[None], norm_gain[None],
            )
        )
    )


def solution(mesh):
    in_specs = (
        P("seq", None),
        P("seq"),
        P(None, "mp"),
        P(None, "mp", None),
        P(None, "mp"),
        P("mp"),
        P("mp"),
        P("mp"),
        P("mp"),
        P("mp", None),
        P("seq", None),
    )
    out_specs = (P("seq", "mp"), P("seq", "mp"))
    return jax.shard_map(
        per_device, mesh=mesh, in_specs=in_specs, out_specs=out_specs, check_vma=False
    )
```
